128 devices in a mesh: dp: 16 (over y, z), ctx: 8 (over x, core).
Axes of the slice: x: 4, y: 4, z: 4, core: 2. Of those that a mesh axis runs over, the one named last changes fastest.
Arguments:
- input_entries: bfloat16 [16, 2048, 8192], P('dp', 'ctx'), may hold values from -6 to 6
- segment_entry_counts: int32 [16, 8, 8], P('dp'), may hold values from 1 to 64, as said below
- segment_destination_part: int32 [16, 8, 8], P('dp'), may hold values from 0 to 7, as said below
- norm_gain: float32 [8192], replicated, may hold values from 0.25 to 1.75
- kv_weight: bfloat16 [8192, 2048], P('dp'), may hold values from -0.0625 to 0.0625
- kv_bias: float32 [2048], replicated, may hold values from -3 to 3
Outputs:
- evened_residual_entries: bfloat16 [16, 2048, 8192], P('dp', 'ctx')
- lookup_stored_tensors: bfloat16 [16, 2048, 2, 8, 128], P('dp', None, None, 'ctx')
The draws below stay inside these ranges and needn't reach their ends.
Inputs may be any that keep to these rules, and one draw needn't show every extreme that they name: `segment_entry_counts`: in each sequence the runs of one shard cover its 256 rows; every shard receives exactly 256 rows; at most 64 rows go from one shard to one shard, and every sequence has a run of exactly 64. The numbers of rows between shards form a Latin arrangement: every shard sends the same list of 8 numbers, one to each shard, and receives each number of that list once. `segment_destination_part`: the 8 runs of one shard go to 8 different shards.
All inputs are finite; a program needn't handle non-finite values.
Results may differ from the reference program's by a relative error of at most 0.0046.
Values may be sent and summed in bfloat16 or wider, within the bound.
A program may use at most 192 MiB of HBM per device.

```python
import jax
import jax.numpy as jnp
from jax import lax

D = 8192
KVH = 8
HD = 128
ROWS = 256
PEERS = 8
BATCH = 16
SEQ = 2048
CAP = 64
COLS = 2048


def plan_draw(key):
    base = jax.random.fold_in(key, 4711)
    peer_count = PEERS
    spare = ROWS - CAP
    share = spare // (peer_count - 1)
    remainder = spare - share * (peer_count - 1)

    def lone_stream(seq_key):
        leading_key, second_key, third_key, fourth_key = jax.random.split(seq_key, 4)
        wobble = jax.random.randint(leading_key, (peer_count - 1,), 0, share // 2 + 1, dtype=jnp.int32)
        shifted = wobble - jnp.roll(wobble, -1)
        extra = (jnp.arange(peer_count - 1, dtype=jnp.int32) < remainder).astype(jnp.int32)
        sizes_list = jnp.concatenate([jnp.full((1,), CAP, jnp.int32), share + shifted + extra])
        row_perm = jax.random.permutation(second_key, peer_count).astype(jnp.int32)
        col_perm = jax.random.permutation(third_key, peer_count).astype(jnp.int32)
        table = sizes_list[(col_perm[None, :] - row_perm[:, None]) % peer_count]
        order_keys = jax.random.split(fourth_key, peer_count)
        orders = jax.vmap(lambda k: jax.random.permutation(k, peer_count).astype(jnp.int32))(order_keys)
        lengths = jnp.take_along_axis(table, orders, axis=1)
        return (lengths, orders)
    seq_keys = jax.random.split(base, BATCH)
    return jax.vmap(lone_stream)(seq_keys)


def draw_segment_entry_counts(key, part):
    lengths, orders = plan_draw(key)
    return lengths


def draw_segment_destination_part(key, part):
    lengths, orders = plan_draw(key)
    return orders


def block_scale(key, dims, cuts, smallest, top_value):
    gain, own = 1.0, jax.random.fold_in(key, 6)
    for dim, blocks in cuts:
        draws = jnp.exp(jax.random.uniform(jax.random.fold_in(own, dim), (blocks,), jnp.float32, smallest / len(cuts), top_value / len(cuts)))
        gain = gain * jnp.repeat(draws, dims[dim] // blocks).reshape([-1 if axis == dim else 1 for axis in range(len(dims))])
    return gain


def scatter_about(rng, extent, width, reach, cuts=(), kind=jnp.bfloat16):
    level = block_scale(rng, extent, cuts, -0.22, 0.18) if cuts else 1.0
    result = jax.random.normal(rng, extent, jnp.float32) * width * level
    return jnp.minimum(jnp.maximum(result, -reach), reach).astype(kind)


def setup_inputs(seed: int = 0) -> dict:
    key_of = jax.random.split(jax.random.key(seed), 7)
    input_entries = scatter_about(key_of[0], (BATCH, SEQ, D), 1.0, 6.0, ((0, 16), (1, 8)))
    segment_entry_counts = draw_segment_entry_counts(jax.random.fold_in(key_of[6], 71), 0)
    segment_destination_part = draw_segment_destination_part(jax.random.fold_in(key_of[6], 71), 0)
    norm_gain = jnp.clip(1.0 + 0.15 * jax.random.normal(key_of[3], (D,), jnp.float32), 0.25, 1.75)
    kv_weight = scatter_about(key_of[4], (D, COLS), D ** -0.5, 0.0625, ((0, 16),))
    kv_bias = scatter_about(key_of[5], (COLS,), 0.5, 3.0, (), jnp.float32)
    return {"input_entries": input_entries, "segment_entry_counts": segment_entry_counts, "segment_destination_part": segment_destination_part, "norm_gain": norm_gain, "kv_weight": kv_weight, "kv_bias": kv_bias}


def plan_tables(lengths, targets, peer_count):
    labels = jnp.arange(peer_count, dtype=jnp.int32)
    starts = jnp.cumsum(lengths, axis=1) - lengths
    matches = (targets[:, :, None] == labels[None, None, :]).astype(jnp.int32)
    counts = lax.optimization_barrier(jnp.sum(lengths[:, :, None] * matches, axis=1))
    anchors = lax.optimization_barrier(jnp.sum(starts[:, :, None] * matches, axis=1))
    run_ends = jnp.cumsum(counts, axis=0)
    offsets = run_ends - counts
    return (counts, anchors, offsets, run_ends)

def source_of(positions, ends_column, offsets_column, anchors_column, peer_count):
    labels = jnp.arange(peer_count, dtype=jnp.int32)
    source = lax.optimization_barrier(jnp.sum((ends_column[None, :] <= positions[:, None]).astype(jnp.int32), axis=1))
    chosen = (source[:, None] == labels[None, :]).astype(jnp.int32)
    within = positions - lax.optimization_barrier(jnp.sum(chosen * offsets_column[None, :], axis=1))
    anchor = lax.optimization_barrier(jnp.sum(chosen * anchors_column[None, :], axis=1))
    return (source, within, anchor)

def reference(input_entries, segment_entry_counts, segment_destination_part, norm_gain, kv_weight, kv_bias):

    def lone_stream(operands):
        sequence, lengths, targets = operands
        counts, anchors, offsets, run_ends = plan_tables(lengths, targets, PEERS)
        positions = jnp.arange(ROWS, dtype=jnp.int32)

        def for_shard(shard):
            source, within, anchor = source_of(positions, run_ends[:, shard], offsets[:, shard], anchors[:, shard], PEERS)
            return source * ROWS + anchor + within
        gather_rows = jax.vmap(for_shard)(jnp.arange(PEERS, dtype=jnp.int32)).reshape(-1)
        moved_rows = jnp.take(sequence, gather_rows, axis=0)
        as_float = moved_rows.astype(jnp.float32)
        inverse_rms = lax.rsqrt(lax.optimization_barrier(jnp.mean(as_float * as_float, axis=-1, keepdims=True)) + 1e-06)
        normed = (as_float * inverse_rms * norm_gain[None, :]).astype(jnp.bfloat16)
        mapped_outputs = jnp.dot(normed, kv_weight, preferred_element_type=jnp.float32) + kv_bias[None, :]
        return (moved_rows, mapped_outputs.astype(jnp.bfloat16).reshape(SEQ, 2, KVH, HD))
    evened_residual_entries, lookup_stored_tensors = lax.map(lone_stream, (input_entries, segment_entry_counts, segment_destination_part))
    return (evened_residual_entries, lookup_stored_tensors)
```

```python
import jax
import jax.numpy as jnp
import numpy as np
from jax import lax
from jax.sharding import Mesh, PartitionSpec as P

KVH = 8
HD = 128


def plan_tables(lengths, targets, peer_count):
    labels = jnp.arange(peer_count, dtype=jnp.int32)
    starts = jnp.cumsum(lengths, axis=1) - lengths
    matches = (targets[:, :, None] == labels[None, None, :]).astype(jnp.int32)
    counts = jnp.sum(lengths[:, :, None] * matches, axis=1)
    anchors = jnp.sum(starts[:, :, None] * matches, axis=1)
    run_ends = jnp.cumsum(counts, axis=0)
    offsets = run_ends - counts
    return (counts, anchors, offsets, run_ends)


def source_of(positions, ends_column, offsets_column, anchors_column, peer_count):
    labels = jnp.arange(peer_count, dtype=jnp.int32)
    source = jnp.sum((ends_column[None, :] <= positions[:, None]).astype(jnp.int32), axis=1)
    chosen = (source[:, None] == labels[None, :]).astype(jnp.int32)
    within = positions - jnp.sum(chosen * offsets_column[None, :], axis=1)
    anchor = jnp.sum(chosen * anchors_column[None, :], axis=1)
    return (source, within, anchor)


def rms_normed(rows, norm_gain):
    as_float = rows.astype(jnp.float32)
    inverse_rms = lax.rsqrt(jnp.mean(as_float * as_float, axis=-1, keepdims=True) + 1e-06)
    return (as_float * inverse_rms * norm_gain[None, :]).astype(jnp.bfloat16)


def pack_document_runs(rows, counts, anchors, myself, peer_count):
    row_count = rows.shape[0]
    capacity = 2 * row_count // peer_count
    slot_index = jnp.arange(capacity, dtype=jnp.int32)
    my_counts = counts[myself]
    my_anchors = anchors[myself]
    wanted = jnp.minimum(my_anchors[:, None] + slot_index[None, :], row_count - 1)
    is_live = slot_index[None, :] < my_counts[:, None]
    picked = jnp.take(rows, wanted.reshape(-1), axis=0).reshape(peer_count, capacity, -1)
    return jnp.where(is_live[:, :, None], picked, jnp.zeros_like(picked))


def unpack_runs(arriving_rows, positions, run_ends, offsets, anchors, myself, peer_count):
    capacity = arriving_rows.shape[1]
    source, within, anchor = source_of(
        positions, run_ends[:, myself], offsets[:, myself], anchors[:, myself], peer_count
    )
    flat_rows = arriving_rows.reshape(peer_count * capacity, -1)
    return jnp.take(flat_rows, source * capacity + within, axis=0)


CTX = ("cx", "cc")


def on_device(
    input_entries, segment_entry_counts, segment_destination_part, norm_gain, kv_weight, kv_bias
):
    chips = lax.axis_size("cx")
    cores = lax.axis_size("cc")
    peer_count = chips * cores
    core = lax.axis_index("cc")
    myself = lax.axis_index("cx") * cores + core
    row_count = input_entries.shape[1]
    width = kv_weight.shape[0]
    heads_per_core = KVH // cores
    local_weight = kv_weight.reshape(width, 2, heads_per_core, cores, HD)
    local_weight = lax.dynamic_index_in_dim(local_weight, core, axis=3, keepdims=False)
    local_weight = local_weight.reshape(width, 2 * heads_per_core * HD)
    local_bias = lax.dynamic_index_in_dim(
        kv_bias.reshape(2, heads_per_core, cores, HD), core, axis=2, keepdims=False
    ).reshape(-1)
    gathered_weight = lax.all_gather(local_weight, "dp", axis=0, tiled=True)

    counts, anchors, offsets, run_ends = plan_tables(
        segment_entry_counts[0], segment_destination_part[0], peer_count
    )
    positions = jnp.arange(row_count, dtype=jnp.int32)
    outgoing = pack_document_runs(input_entries[0], counts, anchors, myself, peer_count)
    arriving_rows = lax.all_to_all(outgoing, CTX, split_axis=0, concat_axis=0, tiled=True)
    moved_rows = unpack_runs(
        arriving_rows, positions, run_ends, offsets, anchors, myself, peer_count
    )
    normed = rms_normed(moved_rows, norm_gain)
    chip_rows = lax.all_gather(normed, "cc", axis=0, tiled=True)
    products = jnp.dot(chip_rows, gathered_weight, preferred_element_type=jnp.float32)
    mapped = (products + local_bias[None, :]).astype(jnp.bfloat16)
    mapped = mapped.reshape(1, cores * row_count, 2, heads_per_core, HD)
    by_heads = lax.all_to_all(mapped, "cx", split_axis=3, concat_axis=1, tiled=True)
    return (moved_rows[None], by_heads)


def solution(mesh):
    dp_size, ctx_size = mesh.devices.shape
    cores = 2
    devices = np.asarray(mesh.devices).reshape(dp_size, ctx_size // cores, cores)
    split_mesh = Mesh(devices, ("dp", "cx", "cc"))
    in_specs = (
        P("dp", CTX, None),
        P("dp", None, None),
        P("dp", None, None),
        P(),
        P("dp", None),
        P(),
    )
    out_specs = (P("dp", CTX, None), P("dp", None, None, CTX, None))
    return jax.shard_map(
        on_device, mesh=split_mesh, in_specs=in_specs, out_specs=out_specs, check_vma=False
    )
```

```python
import jax
import jax.numpy as jnp
import numpy as np
from jax import lax
from jax.sharding import Mesh, PartitionSpec as P

KVH = 8
HD = 128


def plan_tables(lengths, targets, peer_count):
    labels = jnp.arange(peer_count, dtype=jnp.int32)
    starts = jnp.cumsum(lengths, axis=1) - lengths
    matches = (targets[:, :, None] == labels[None, None, :]).astype(jnp.int32)
    counts = jnp.sum(lengths[:, :, None] * matches, axis=1)
    anchors = jnp.sum(starts[:, :, None] * matches, axis=1)
    run_ends = jnp.cumsum(counts, axis=0)
    offsets = run_ends - counts
    return (counts, anchors, offsets, run_ends)


def source_of(positions, ends_column, offsets_column, anchors_column, peer_count):
    labels = jnp.arange(peer_count, dtype=jnp.int32)
    source = jnp.sum((ends_column[None, :] <= positions[:, None]).astype(jnp.int32), axis=1)
    chosen = (source[:, None] == labels[None, :]).astype(jnp.int32)
    within = positions - jnp.sum(chosen * offsets_column[None, :], axis=1)
    anchor = jnp.sum(chosen * anchors_column[None, :], axis=1)
    return (source, within, anchor)


def rms_normed(rows, norm_gain):
    as_float = rows.astype(jnp.float32)
    inverse_rms = lax.rsqrt(jnp.mean(as_float * as_float, axis=-1, keepdims=True) + 1e-06)
    return (as_float * inverse_rms * norm_gain[None, :]).astype(jnp.bfloat16)


def pack_document_runs(rows, counts, anchors, myself, peer_count):
    row_count = rows.shape[0]
    capacity = 2 * row_count // peer_count
    slot_index = jnp.arange(capacity, dtype=jnp.int32)
    my_counts = counts[myself]
    my_anchors = anchors[myself]
    wanted = jnp.minimum(my_anchors[:, None] + slot_index[None, :], row_count - 1)
    is_live = slot_index[None, :] < my_counts[:, None]
    picked = jnp.take(rows, wanted.reshape(-1), axis=0).reshape(peer_count, capacity, -1)
    return jnp.where(is_live[:, :, None], picked, jnp.zeros_like(picked))


def unpack_runs(arriving_rows, positions, run_ends, offsets, anchors, myself, peer_count):
    capacity = arriving_rows.shape[1]
    source, within, anchor = source_of(
        positions, run_ends[:, myself], offsets[:, myself], anchors[:, myself], peer_count
    )
    flat_rows = arriving_rows.reshape(peer_count * capacity, -1)
    return jnp.take(flat_rows, source * capacity + within, axis=0)


CTX = ("cx", "cc")


def on_device(
    input_entries, segment_entry_counts, segment_destination_part, norm_gain, kv_weight, kv_bias
):
    chips = lax.axis_size("cx")
    cores = lax.axis_size("cc")
    peer_count = chips * cores
    core = lax.axis_index("cc")
    myself = lax.axis_index("cx") * cores + core
    row_count = input_entries.shape[1]
    width = kv_weight.shape[0]
    heads_per_core = KVH // cores
    local_weight = kv_weight.reshape(width, 2, heads_per_core, cores, HD)
    local_weight = lax.dynamic_index_in_dim(local_weight, core, axis=3, keepdims=False)
    local_weight = local_weight.reshape(width, 2 * heads_per_core * HD)
    local_bias = lax.dynamic_index_in_dim(
        kv_bias.reshape(2, heads_per_core, cores, HD), core, axis=2, keepdims=False
    ).reshape(-1)
    local_weight, local_bias, input_entries = lax.optimization_barrier(
        (local_weight, local_bias, input_entries)
    )
    gathered_weight = lax.all_gather(local_weight, "dp", axis=0, tiled=True)

    counts, anchors, offsets, run_ends = plan_tables(
        segment_entry_counts[0], segment_destination_part[0], peer_count
    )
    positions = jnp.arange(row_count, dtype=jnp.int32)
    outgoing = pack_document_runs(input_entries[0], counts, anchors, myself, peer_count)
    arriving_rows = lax.all_to_all(outgoing, CTX, split_axis=0, concat_axis=0, tiled=True)
    moved_rows = unpack_runs(
        arriving_rows, positions, run_ends, offsets, anchors, myself, peer_count
    )
    normed = rms_normed(moved_rows, norm_gain)
    sibling_rows = lax.ppermute(normed, "cc", perm=[(0, 1), (1, 0)])

    def project(rows):
        products = jnp.dot(rows, gathered_weight, preferred_element_type=jnp.float32)
        return (products + local_bias[None, :]).astype(jnp.bfloat16)

    own = project(normed)
    other = project(sibling_rows)
    first = jnp.where(core == 0, own, other)
    second = jnp.where(core == 0, other, own)
    mapped = jnp.concatenate([first, second], axis=0)
    mapped = mapped.reshape(1, cores * row_count, 2, heads_per_core, HD)
    by_heads = lax.all_to_all(mapped, "cx", split_axis=3, concat_axis=1, tiled=True)
    return (moved_rows[None], by_heads)


def solution(mesh):
    dp_size, ctx_size = mesh.devices.shape
    cores = 2
    devices = np.asarray(mesh.devices).reshape(dp_size, ctx_size // cores, cores)
    split_mesh = Mesh(devices, ("dp", "cx", "cc"))
    in_specs = (
        P("dp", CTX, None),
        P("dp", None, None),
        P("dp", None, None),
        P(),
        P("dp", None),
        P(),
    )
    out_specs = (P("dp", CTX, None), P("dp", None, None, CTX, None))
    return jax.shard_map(
        on_device, mesh=split_mesh, in_specs=in_specs, out_specs=out_specs, check_vma=False
    )
```

```python
import jax
import jax.numpy as jnp
import numpy as np
from jax import lax
from jax.sharding import Mesh, PartitionSpec as P

KVH = 8
HD = 128


def plan_tables(lengths, targets, peer_count):
    labels = jnp.arange(peer_count, dtype=jnp.int32)
    starts = jnp.cumsum(lengths, axis=1) - lengths
    matches = (targets[:, :, None] == labels[None, None, :]).astype(jnp.int32)
    counts = jnp.sum(lengths[:, :, None] * matches, axis=1)
    anchors = jnp.sum(starts[:, :, None] * matches, axis=1)
    run_ends = jnp.cumsum(counts, axis=0)
    offsets = run_ends - counts
    return (counts, anchors, offsets, run_ends)


def source_of(positions, ends_column, offsets_column, anchors_column, peer_count):
    labels = jnp.arange(peer_count, dtype=jnp.int32)
    source = jnp.sum((ends_column[None, :] <= positions[:, None]).astype(jnp.int32), axis=1)
    chosen = (source[:, None] == labels[None, :]).astype(jnp.int32)
    within = positions - jnp.sum(chosen * offsets_column[None, :], axis=1)
    anchor = jnp.sum(chosen * anchors_column[None, :], axis=1)
    return (source, within, anchor)


def rms_normed(rows, norm_gain):
    as_float = rows.astype(jnp.float32)
    inverse_rms = lax.rsqrt(jnp.mean(as_float * as_float, axis=-1, keepdims=True) + 1e-06)
    return (as_float * inverse_rms * norm_gain[None, :]).astype(jnp.bfloat16)


def pack_document_runs(rows, counts, anchors, myself, peer_count):
    row_count = rows.shape[0]
    capacity = 2 * row_count // peer_count
    slot_index = jnp.arange(capacity, dtype=jnp.int32)
    my_anchors = anchors[myself]
    wanted = jnp.minimum(my_anchors[:, None] + slot_index[None, :], row_count - 1)
    return jnp.take(rows, wanted.reshape(-1), axis=0, mode="clip").reshape(peer_count, capacity, -1)


def unpack_runs(arriving_rows, positions, run_ends, offsets, anchors, myself, peer_count):
    capacity = arriving_rows.shape[1]
    source, within, anchor = source_of(
        positions, run_ends[:, myself], offsets[:, myself], anchors[:, myself], peer_count
    )
    flat_rows = arriving_rows.reshape(peer_count * capacity, -1)
    return jnp.take(flat_rows, source * capacity + within, axis=0, mode="clip")


def gather_map(run_ends, offsets, anchors, row_count, peer_count):
    positions = jnp.arange(row_count, dtype=jnp.int32)

    def for_shard(shard):
        source, within, anchor = source_of(
            positions, run_ends[:, shard], offsets[:, shard], anchors[:, shard], peer_count
        )
        return source * row_count + anchor + within

    return jax.vmap(for_shard)(jnp.arange(peer_count, dtype=jnp.int32)).reshape(-1)


CTX = ("cx", "cc")


def on_device(
    input_entries, segment_entry_counts, segment_destination_part, norm_gain, kv_weight, kv_bias
):
    chips = lax.axis_size("cx")
    cores = lax.axis_size("cc")
    peer_count = chips * cores
    core = lax.axis_index("cc")
    myself = lax.axis_index("cx") * cores + core
    row_count = input_entries.shape[1]
    width = kv_weight.shape[0]
    heads_per_core = KVH // cores
    local_weight = kv_weight.reshape(width, 2, heads_per_core, cores, HD)
    local_weight = lax.dynamic_index_in_dim(local_weight, core, axis=3, keepdims=False)
    local_weight = jnp.transpose(local_weight, (2, 0, 1, 3)).reshape(
        heads_per_core, width, 2 * HD
    )
    local_bias = lax.dynamic_index_in_dim(
        kv_bias.reshape(2, heads_per_core, cores, HD), core, axis=2, keepdims=False
    )
    local_bias = jnp.transpose(local_bias, (1, 0, 2)).reshape(heads_per_core, 2 * HD)
    local_weight, local_bias, input_entries = lax.optimization_barrier(
        (local_weight, local_bias, input_entries)
    )
    rows = input_entries[0]

    normed = rms_normed(rows, norm_gain)
    sibling_rows = lax.ppermute(normed, "cc", perm=[(0, 1), (1, 0)])
    blocks = []
    for head in range(heads_per_core):
        head_weight = lax.all_gather(local_weight[head], "dp", axis=0, tiled=True)
        own = jnp.dot(normed, head_weight, preferred_element_type=jnp.float32)
        other = jnp.dot(sibling_rows, head_weight, preferred_element_type=jnp.float32)
        own = (own + local_bias[head][None, :]).astype(jnp.bfloat16)
        other = (other + local_bias[head][None, :]).astype(jnp.bfloat16)
        first = jnp.where(core == 0, own, other)
        second = jnp.where(core == 0, other, own)
        blocks.append(jnp.concatenate([first, second], axis=0))
    mapped = jnp.stack(blocks, axis=1).reshape(1, cores * row_count, heads_per_core, 2, HD)
    by_heads = lax.all_to_all(mapped, "cx", split_axis=2, concat_axis=1, tiled=True)

    counts, anchors, offsets, run_ends = plan_tables(
        segment_entry_counts[0], segment_destination_part[0], peer_count
    )
    positions = jnp.arange(row_count, dtype=jnp.int32)
    outgoing = pack_document_runs(rows, counts, anchors, myself, peer_count)
    arriving_rows = lax.all_to_all(outgoing, CTX, split_axis=0, concat_axis=0, tiled=True)
    moved_rows = unpack_runs(
        arriving_rows, positions, run_ends, offsets, anchors, myself, peer_count
    )
    order = gather_map(run_ends, offsets, anchors, row_count, peer_count)
    evened = jnp.take(by_heads.reshape(peer_count * row_count, 2, HD), order, axis=0, mode="clip")
    return (moved_rows[None], evened.reshape(1, peer_count * row_count, 2, 1, HD))


def solution(mesh):
    dp_size, ctx_size = mesh.devices.shape
    cores = 2
    devices = np.asarray(mesh.devices).reshape(dp_size, ctx_size // cores, cores)
    split_mesh = Mesh(devices, ("dp", "cx", "cc"))
    in_specs = (
        P("dp", CTX, None),
        P("dp", None, None),
        P("dp", None, None),
        P(),
        P("dp", None),
        P(),
    )
    out_specs = (P("dp", CTX, None), P("dp", None, None, CTX, None))
    return jax.shard_map(
        on_device, mesh=split_mesh, in_specs=in_specs, out_specs=out_specs, check_vma=False
    )
```

```python
import jax
import jax.numpy as jnp
import numpy as np
from jax import lax
from jax.sharding import Mesh, PartitionSpec as P

KVH = 8
HD = 128


def plan_tables(lengths, targets, peer_count):
    labels = jnp.arange(peer_count, dtype=jnp.int32)
    starts = jnp.cumsum(lengths, axis=1) - lengths
    matches = (targets[:, :, None] == labels[None, None, :]).astype(jnp.int32)
    counts = jnp.sum(lengths[:, :, None] * matches, axis=1)
    anchors = jnp.sum(starts[:, :, None] * matches, axis=1)
    run_ends = jnp.cumsum(counts, axis=0)
    offsets = run_ends - counts
    return (counts, anchors, offsets, run_ends)


def source_of(positions, ends_column, offsets_column, anchors_column, peer_count):
    labels = jnp.arange(peer_count, dtype=jnp.int32)
    source = jnp.sum((ends_column[None, :] <= positions[:, None]).astype(jnp.int32), axis=1)
    chosen = (source[:, None] == labels[None, :]).astype(jnp.int32)
    within = positions - jnp.sum(chosen * offsets_column[None, :], axis=1)
    anchor = jnp.sum(chosen * anchors_column[None, :], axis=1)
    return (source, within, anchor)


def rms_normed(rows, norm_gain):
    as_float = rows.astype(jnp.float32)
    inverse_rms = lax.rsqrt(jnp.mean(as_float * as_float, axis=-1, keepdims=True) + 1e-06)
    return (as_float * inverse_rms * norm_gain[None, :]).astype(jnp.bfloat16)


def pack_document_runs(rows, counts, anchors, myself, peer_count):
    row_count = rows.shape[0]
    capacity = 2 * row_count // peer_count
    slot_index = jnp.arange(capacity, dtype=jnp.int32)
    my_anchors = anchors[myself]
    wanted = jnp.minimum(my_anchors[:, None] + slot_index[None, :], row_count - 1)
    return jnp.take(rows, wanted.reshape(-1), axis=0, mode="clip").reshape(peer_count, capacity, -1)


def unpack_runs(arriving_rows, positions, run_ends, offsets, anchors, myself, peer_count):
    capacity = arriving_rows.shape[1]
    source, within, anchor = source_of(
        positions, run_ends[:, myself], offsets[:, myself], anchors[:, myself], peer_count
    )
    flat_rows = arriving_rows.reshape(peer_count * capacity, -1)
    return jnp.take(flat_rows, source * capacity + within, axis=0, mode="clip")


def gather_map(run_ends, offsets, anchors, row_count, peer_count):
    positions = jnp.arange(row_count, dtype=jnp.int32)

    def for_shard(shard):
        source, within, anchor = source_of(
            positions, run_ends[:, shard], offsets[:, shard], anchors[:, shard], peer_count
        )
        return source * row_count + anchor + within

    return jax.vmap(for_shard)(jnp.arange(peer_count, dtype=jnp.int32)).reshape(-1)


CTX = ("cx", "cc")
DP = ("dy", "dz")


def shift(x, axis, step):
    n = lax.axis_size(axis)
    return lax.ppermute(x, axis, perm=[(i, (i + step) % n) for i in range(n)])


def ring_gather(x, axis):
    from_prev = shift(x, axis, 1)
    from_next = shift(x, axis, -1)
    half = x.shape[-1] // 2
    far_lo = shift(from_prev[..., :half], axis, 1)
    far_hi = shift(from_next[..., half:], axis, -1)
    far = jnp.concatenate([far_lo, far_hi], axis=-1)
    return jnp.stack([x, from_next, far, from_prev], axis=0)


def on_device(
    input_entries, segment_entry_counts, segment_destination_part, norm_gain, kv_weight, kv_bias
):
    chips = lax.axis_size("cx")
    cores = lax.axis_size("cc")
    peer_count = chips * cores
    core = lax.axis_index("cc")
    myself = lax.axis_index("cx") * cores + core
    row_count = input_entries.shape[1]
    piece = kv_weight.shape[0]
    width = norm_gain.shape[0]
    heads_per_core = KVH // cores
    n_y = lax.axis_size("dy")
    n_z = lax.axis_size("dz")
    my_y = lax.axis_index("dy")
    my_z = lax.axis_index("dz")
    local_weight = kv_weight.reshape(piece, 2, heads_per_core, cores, HD)
    local_weight = lax.dynamic_index_in_dim(local_weight, core, axis=3, keepdims=False)
    local_weight = local_weight.reshape(piece, 2, heads_per_core * HD)
    local_bias = lax.dynamic_index_in_dim(
        kv_bias.reshape(2, heads_per_core, cores, HD), core, axis=2, keepdims=False
    )
    local_weight, local_bias, input_entries = lax.optimization_barrier(
        (local_weight, local_bias, input_entries)
    )
    rows = input_entries[0]

    key_weight = ring_gather(ring_gather(local_weight[:, 0], "dz"), "dy")
    value_weight = ring_gather(ring_gather(local_weight[:, 1], "dy"), "dz")
    key_weight = key_weight.reshape(width, heads_per_core * HD)
    value_weight = value_weight.reshape(width, heads_per_core * HD)

    normed = rms_normed(rows, norm_gain).reshape(row_count, n_y, n_z, piece)
    normed = jnp.roll(jnp.roll(normed, -my_y, axis=1), -my_z, axis=2)
    own_key_rows = normed.reshape(row_count, width)
    own_value_rows = jnp.swapaxes(normed, 1, 2).reshape(row_count, width)
    sib_key_rows = lax.ppermute(own_key_rows, "cc", perm=[(0, 1), (1, 0)])
    sib_value_rows = lax.ppermute(own_value_rows, "cc", perm=[(0, 1), (1, 0)])
    bias = jnp.swapaxes(local_bias, 0, 1)

    def project(key_rows, value_rows):
        keys = jnp.dot(key_rows, key_weight, preferred_element_type=jnp.float32)
        values = jnp.dot(value_rows, value_weight, preferred_element_type=jnp.float32)
        both = jnp.stack(
            [keys.reshape(row_count, heads_per_core, HD), values.reshape(row_count, heads_per_core, HD)],
            axis=2,
        )
        return (both + bias[None]).astype(jnp.bfloat16)

    own = project(own_key_rows, own_value_rows)
    other = project(sib_key_rows, sib_value_rows)
    first = jnp.where(core == 0, own, other)
    second = jnp.where(core == 0, other, own)
    mapped = jnp.concatenate([first, second], axis=0)[None]
    by_heads = lax.all_to_all(mapped, "cx", split_axis=2, concat_axis=1, tiled=True)

    counts, anchors, offsets, run_ends = plan_tables(
        segment_entry_counts[0], segment_destination_part[0], peer_count
    )
    positions = jnp.arange(row_count, dtype=jnp.int32)
    outgoing = pack_document_runs(rows, counts, anchors, myself, peer_count)
    arriving_rows = lax.all_to_all(outgoing, CTX, split_axis=0, concat_axis=0, tiled=True)
    moved_rows = unpack_runs(
        arriving_rows, positions, run_ends, offsets, anchors, myself, peer_count
    )
    order = gather_map(run_ends, offsets, anchors, row_count, peer_count)
    evened = jnp.take(by_heads.reshape(peer_count * row_count, 2, HD), order, axis=0, mode="clip")
    return (moved_rows[None], evened.reshape(1, peer_count * row_count, 2, 1, HD))


def solution(mesh):
    dp_size, ctx_size = mesh.devices.shape
    cores = 2
    sides = 4
    devices = np.asarray(mesh.devices).reshape(sides, dp_size // sides, ctx_size // cores, cores)
    split_mesh = Mesh(devices, ("dy", "dz", "cx", "cc"))
    in_specs = (
        P(DP, CTX, None),
        P(DP, None, None),
        P(DP, None, None),
        P(),
        P(DP, None),
        P(),
    )
    out_specs = (P(DP, CTX, None), P(DP, None, None, CTX, None))
    return jax.shard_map(
        on_device, mesh=split_mesh, in_specs=in_specs, out_specs=out_specs, check_vma=False
    )
```

```python
import jax
import jax.numpy as jnp
import numpy as np
from jax import lax
from jax.experimental import pallas as pl
from jax.experimental.pallas import tpu as pltpu
from jax.sharding import Mesh, PartitionSpec as P

KVH = 8
HD = 128


def plan_tables(lengths, targets, peer_count):
    labels = jnp.arange(peer_count, dtype=jnp.int32)
    starts = jnp.cumsum(lengths, axis=1) - lengths
    matches = (targets[:, :, None] == labels[None, None, :]).astype(jnp.int32)
    counts = jnp.sum(lengths[:, :, None] * matches, axis=1)
    anchors = jnp.sum(starts[:, :, None] * matches, axis=1)
    run_ends = jnp.cumsum(counts, axis=0)
    offsets = run_ends - counts
    return (counts, anchors, offsets, run_ends)


def source_of(positions, ends_column, offsets_column, anchors_column, peer_count):
    labels = jnp.arange(peer_count, dtype=jnp.int32)
    source = jnp.sum((ends_column[None, :] <= positions[:, None]).astype(jnp.int32), axis=1)
    chosen = (source[:, None] == labels[None, :]).astype(jnp.int32)
    within = positions - jnp.sum(chosen * offsets_column[None, :], axis=1)
    anchor = jnp.sum(chosen * anchors_column[None, :], axis=1)
    return (source, within, anchor)


def rms_normed(rows, norm_gain):
    as_float = rows.astype(jnp.float32)
    inverse_rms = lax.rsqrt(jnp.mean(as_float * as_float, axis=-1, keepdims=True) + 1e-06)
    return (as_float * inverse_rms * norm_gain[None, :]).astype(jnp.bfloat16)


def window_starts(anchors, row_count, capacity):
    return jnp.minimum(anchors, row_count - capacity)


def _pack_kernel(starts_ref, rows_hbm, out_hbm, sems):
    peer_count, capacity = out_hbm.shape[0], out_hbm.shape[1]
    copies = [
        pltpu.make_async_copy(
            rows_hbm.at[pl.ds(starts_ref[k], capacity)], out_hbm.at[k], sems.at[k]
        )
        for k in range(peer_count)
    ]
    for copy in copies:
        copy.start()
    for copy in copies:
        copy.wait()


def pack_document_runs(rows, starts, peer_count, capacity):
    return pl.pallas_call(
        _pack_kernel,
        out_shape=jax.ShapeDtypeStruct((peer_count, capacity) + rows.shape[1:], rows.dtype),
        grid_spec=pltpu.PrefetchScalarGridSpec(
            num_scalar_prefetch=1,
            grid=(1,),
            in_specs=[pl.BlockSpec(memory_space=pl.ANY)],
            out_specs=pl.BlockSpec(memory_space=pl.ANY),
            scratch_shapes=[pltpu.SemaphoreType.DMA((peer_count,))],
        ),
    )(starts, rows)


def _unpack_kernel(index_ref, flat_hbm, out_hbm, sem):
    row_count = out_hbm.shape[0]

    def start_row(p, carry):
        pltpu.make_async_copy(
            flat_hbm.at[pl.ds(index_ref[p], 1)], out_hbm.at[pl.ds(p, 1)], sem.at[0]
        ).start()
        return carry

    lax.fori_loop(0, row_count, start_row, 0)
    pltpu.make_async_copy(flat_hbm.at[pl.ds(0, row_count)], out_hbm, sem.at[0]).wait()


def unpack_runs(flat_rows, index, row_count):
    return pl.pallas_call(
        _unpack_kernel,
        out_shape=jax.ShapeDtypeStruct((row_count,) + flat_rows.shape[1:], flat_rows.dtype),
        grid_spec=pltpu.PrefetchScalarGridSpec(
            num_scalar_prefetch=1,
            grid=(1,),
            in_specs=[pl.BlockSpec(memory_space=pl.ANY)],
            out_specs=pl.BlockSpec(memory_space=pl.ANY),
            scratch_shapes=[pltpu.SemaphoreType.DMA((1,))],
        ),
    )(index, flat_rows)


CTX = ("cx", "cc")


def on_device(
    input_entries, segment_entry_counts, segment_destination_part, norm_gain, kv_weight, kv_bias
):
    chips = lax.axis_size("cx")
    cores = lax.axis_size("cc")
    peer_count = chips * cores
    core = lax.axis_index("cc")
    myself = lax.axis_index("cx") * cores + core
    row_count = input_entries.shape[1]
    width = kv_weight.shape[0]
    heads_per_core = KVH // cores
    local_weight = kv_weight.reshape(width, 2, heads_per_core, cores, HD)
    local_weight = lax.dynamic_index_in_dim(local_weight, core, axis=3, keepdims=False)
    local_weight = local_weight.reshape(width, 2 * heads_per_core * HD)
    local_bias = lax.dynamic_index_in_dim(
        kv_bias.reshape(2, heads_per_core, cores, HD), core, axis=2, keepdims=False
    ).reshape(-1)
    local_weight, local_bias, input_entries = lax.optimization_barrier(
        (local_weight, local_bias, input_entries)
    )
    gathered_weight = lax.all_gather(local_weight, "dp", axis=0, tiled=True)

    counts, anchors, offsets, run_ends = plan_tables(
        segment_entry_counts[0], segment_destination_part[0], peer_count
    )
    positions = jnp.arange(row_count, dtype=jnp.int32)
    capacity = 2 * row_count // peer_count
    starts = window_starts(anchors, row_count, capacity)
    lanes = 128
    width = input_entries.shape[2]
    row_blocks = input_entries[0].reshape(row_count, width // lanes, lanes)
    outgoing = pack_document_runs(row_blocks, starts[myself], peer_count, capacity)
    arriving_rows = lax.all_to_all(outgoing, CTX, split_axis=0, concat_axis=0, tiled=True)
    source, within, anchor = source_of(
        positions, run_ends[:, myself], offsets[:, myself], anchors[:, myself], peer_count
    )
    shift = anchor - jnp.take(starts[:, myself], source, mode="clip")
    index = source * capacity + shift + within
    moved_rows = unpack_runs(
        arriving_rows.reshape((peer_count * capacity,) + row_blocks.shape[1:]), index, row_count
    ).reshape(row_count, width)
    normed = rms_normed(moved_rows, norm_gain)
    sibling_rows = lax.ppermute(normed, "cc", perm=[(0, 1), (1, 0)])

    def project(rows):
        products = jnp.dot(rows, gathered_weight, preferred_element_type=jnp.float32)
        return (products + local_bias[None, :]).astype(jnp.bfloat16)

    own = project(normed)
    other = project(sibling_rows)
    first = jnp.where(core == 0, own, other)
    second = jnp.where(core == 0, other, own)
    mapped = jnp.concatenate([first, second], axis=0)
    mapped = mapped.reshape(1, cores * row_count, 2, heads_per_core, HD)
    by_heads = lax.all_to_all(mapped, "cx", split_axis=3, concat_axis=1, tiled=True)
    return (moved_rows[None], by_heads)


def solution(mesh):
    dp_size, ctx_size = mesh.devices.shape
    cores = 2
    devices = np.asarray(mesh.devices).reshape(dp_size, ctx_size // cores, cores)
    split_mesh = Mesh(devices, ("dp", "cx", "cc"))
    in_specs = (
        P("dp", CTX, None),
        P("dp", None, None),
        P("dp", None, None),
        P(),
        P("dp", None),
        P(),
    )
    out_specs = (P("dp", CTX, None), P("dp", None, None, CTX, None))
    return jax.shard_map(
        on_device, mesh=split_mesh, in_specs=in_specs, out_specs=out_specs, check_vma=False
    )
```

```python
import jax
import jax.numpy as jnp
import numpy as np
from jax import lax
from jax.experimental import pallas as pl
from jax.experimental.pallas import tpu as pltpu
from jax.sharding import Mesh, PartitionSpec as P

KVH = 8
HD = 128


def plan_tables(lengths, targets, peer_count):
    labels = jnp.arange(peer_count, dtype=jnp.int32)
    starts = jnp.cumsum(lengths, axis=1) - lengths
    matches = (targets[:, :, None] == labels[None, None, :]).astype(jnp.int32)
    counts = jnp.sum(lengths[:, :, None] * matches, axis=1)
    anchors = jnp.sum(starts[:, :, None] * matches, axis=1)
    run_ends = jnp.cumsum(counts, axis=0)
    offsets = run_ends - counts
    return (counts, anchors, offsets, run_ends)


def source_of(positions, ends_column, offsets_column, anchors_column, peer_count):
    labels = jnp.arange(peer_count, dtype=jnp.int32)
    source = jnp.sum((ends_column[None, :] <= positions[:, None]).astype(jnp.int32), axis=1)
    chosen = (source[:, None] == labels[None, :]).astype(jnp.int32)
    within = positions - jnp.sum(chosen * offsets_column[None, :], axis=1)
    anchor = jnp.sum(chosen * anchors_column[None, :], axis=1)
    return (source, within, anchor)


def rms_normed(rows, norm_gain):
    as_float = rows.astype(jnp.float32)
    inverse_rms = lax.rsqrt(jnp.mean(as_float * as_float, axis=-1, keepdims=True) + 1e-06)
    return (as_float * inverse_rms * norm_gain[None, :]).astype(jnp.bfloat16)


def window_starts(anchors, row_count, capacity):
    return jnp.minimum(anchors, row_count - capacity)


def _pack_kernel(starts_ref, rows_ref, out_ref):
    peer_count, capacity = out_ref.shape[0], out_ref.shape[1]
    for k in range(peer_count):
        out_ref[k] = rows_ref[pl.ds(starts_ref[k], capacity)]


def _whole(shape):
    return pl.BlockSpec(shape, lambda i, *_: (0,) * len(shape))


def pack_document_runs(rows, starts, peer_count, capacity):
    out_shape = (peer_count, capacity) + rows.shape[1:]
    return pl.pallas_call(
        _pack_kernel,
        out_shape=jax.ShapeDtypeStruct(out_shape, rows.dtype),
        grid_spec=pltpu.PrefetchScalarGridSpec(
            num_scalar_prefetch=1,
            grid=(1,),
            in_specs=[_whole(rows.shape)],
            out_specs=_whole(out_shape),
        ),
    )(starts, rows)


def _unpack_kernel(index_ref, flat_ref, out_ref):
    def move_row(p, carry):
        out_ref[p] = flat_ref[index_ref[p]]
        return carry

    lax.fori_loop(0, out_ref.shape[0], move_row, 0, unroll=8)


def unpack_runs(flat_rows, index, row_count):
    out_shape = (row_count,) + flat_rows.shape[1:]
    return pl.pallas_call(
        _unpack_kernel,
        out_shape=jax.ShapeDtypeStruct(out_shape, flat_rows.dtype),
        grid_spec=pltpu.PrefetchScalarGridSpec(
            num_scalar_prefetch=1,
            grid=(1,),
            in_specs=[_whole(flat_rows.shape)],
            out_specs=_whole(out_shape),
        ),
    )(index, flat_rows)


CTX = ("cx", "cc")


def on_device(
    input_entries, segment_entry_counts, segment_destination_part, norm_gain, kv_weight, kv_bias
):
    chips = lax.axis_size("cx")
    cores = lax.axis_size("cc")
    peer_count = chips * cores
    core = lax.axis_index("cc")
    myself = lax.axis_index("cx") * cores + core
    row_count = input_entries.shape[1]
    width = kv_weight.shape[0]
    heads_per_core = KVH // cores
    local_weight = kv_weight.reshape(width, 2, heads_per_core, cores, HD)
    local_weight = lax.dynamic_index_in_dim(local_weight, core, axis=3, keepdims=False)
    local_weight = local_weight.reshape(width, 2 * heads_per_core * HD)
    local_bias = lax.dynamic_index_in_dim(
        kv_bias.reshape(2, heads_per_core, cores, HD), core, axis=2, keepdims=False
    ).reshape(-1)
    local_weight, local_bias, input_entries = lax.optimization_barrier(
        (local_weight, local_bias, input_entries)
    )
    gathered_weight = lax.all_gather(local_weight, "dp", axis=0, tiled=True)

    counts, anchors, offsets, run_ends = plan_tables(
        segment_entry_counts[0], segment_destination_part[0], peer_count
    )
    positions = jnp.arange(row_count, dtype=jnp.int32)
    capacity = 2 * row_count // peer_count
    starts = window_starts(anchors, row_count, capacity)
    lanes = 128
    width = input_entries.shape[2]
    row_blocks = input_entries[0].reshape(row_count, width // lanes, lanes)
    outgoing = pack_document_runs(row_blocks, starts[myself], peer_count, capacity)
    arriving_rows = lax.all_to_all(outgoing, CTX, split_axis=0, concat_axis=0, tiled=True)
    source, within, anchor = source_of(
        positions, run_ends[:, myself], offsets[:, myself], anchors[:, myself], peer_count
    )
    shift = anchor - jnp.take(starts[:, myself], source, mode="clip")
    index = source * capacity + shift + within
    moved_rows = unpack_runs(
        arriving_rows.reshape((peer_count * capacity,) + row_blocks.shape[1:]), index, row_count
    ).reshape(row_count, width)
    normed = rms_normed(moved_rows, norm_gain)
    sibling_rows = lax.ppermute(normed, "cc", perm=[(0, 1), (1, 0)])

    def project(rows):
        products = jnp.dot(rows, gathered_weight, preferred_element_type=jnp.float32)
        return (products + local_bias[None, :]).astype(jnp.bfloat16)

    own = project(normed)
    other = project(sibling_rows)
    first = jnp.where(core == 0, own, other)
    second = jnp.where(core == 0, other, own)
    mapped = jnp.concatenate([first, second], axis=0)
    mapped = mapped.reshape(1, cores * row_count, 2, heads_per_core, HD)
    by_heads = lax.all_to_all(mapped, "cx", split_axis=3, concat_axis=1, tiled=True)
    return (moved_rows[None], by_heads)


def solution(mesh):
    dp_size, ctx_size = mesh.devices.shape
    cores = 2
    devices = np.asarray(mesh.devices).reshape(dp_size, ctx_size // cores, cores)
    split_mesh = Mesh(devices, ("dp", "cx", "cc"))
    in_specs = (
        P("dp", CTX, None),
        P("dp", None, None),
        P("dp", None, None),
        P(),
        P("dp", None),
        P(),
    )
    out_specs = (P("dp", CTX, None), P("dp", None, None, CTX, None))
    return jax.shard_map(
        on_device, mesh=split_mesh, in_specs=in_specs, out_specs=out_specs, check_vma=False
    )
```

```python
import jax
import jax.numpy as jnp
import numpy as np
from jax import lax
from jax.experimental import pallas as pl
from jax.experimental.pallas import tpu as pltpu
from jax.sharding import Mesh, PartitionSpec as P

KVH = 8
HD = 128


def plan_tables(lengths, targets, peer_count):
    labels = jnp.arange(peer_count, dtype=jnp.int32)
    starts = jnp.cumsum(lengths, axis=1) - lengths
    matches = (targets[:, :, None] == labels[None, None, :]).astype(jnp.int32)
    counts = jnp.sum(lengths[:, :, None] * matches, axis=1)
    anchors = jnp.sum(starts[:, :, None] * matches, axis=1)
    run_ends = jnp.cumsum(counts, axis=0)
    offsets = run_ends - counts
    return (counts, anchors, offsets, run_ends)


def source_of(positions, ends_column, offsets_column, anchors_column, peer_count):
    labels = jnp.arange(peer_count, dtype=jnp.int32)
    source = jnp.sum((ends_column[None, :] <= positions[:, None]).astype(jnp.int32), axis=1)
    chosen = (source[:, None] == labels[None, :]).astype(jnp.int32)
    within = positions - jnp.sum(chosen * offsets_column[None, :], axis=1)
    anchor = jnp.sum(chosen * anchors_column[None, :], axis=1)
    return (source, within, anchor)


def rms_normed(rows, norm_gain):
    as_float = rows.astype(jnp.float32)
    inverse_rms = lax.rsqrt(jnp.mean(as_float * as_float, axis=-1, keepdims=True) + 1e-06)
    return (as_float * inverse_rms * norm_gain[None, :]).astype(jnp.bfloat16)


def window_starts(anchors, row_count, capacity):
    return jnp.minimum(anchors, row_count - capacity)


def _pack_kernel(starts_ref, rows_ref, out_ref):
    peer_count, capacity = out_ref.shape[0], out_ref.shape[1]
    for k in range(peer_count):
        out_ref[k] = rows_ref[pl.ds(starts_ref[k], capacity)]


def _whole(shape):
    return pl.BlockSpec(shape, lambda i, *_: (0,) * len(shape))


def pack_document_runs(rows, starts, peer_count, capacity):
    out_shape = (peer_count, capacity) + rows.shape[1:]
    return pl.pallas_call(
        _pack_kernel,
        out_shape=jax.ShapeDtypeStruct(out_shape, rows.dtype),
        grid_spec=pltpu.PrefetchScalarGridSpec(
            num_scalar_prefetch=1,
            grid=(1,),
            in_specs=[_whole(rows.shape)],
            out_specs=_whole(out_shape),
        ),
    )(starts, rows)


def _unpack_kernel(index_ref, flat_ref, out_ref):
    def move_row(p, carry):
        out_ref[p] = flat_ref[index_ref[p]]
        return carry

    lax.fori_loop(0, out_ref.shape[0], move_row, 0, unroll=8)


def unpack_runs(flat_rows, index, row_count):
    out_shape = (row_count,) + flat_rows.shape[1:]
    return pl.pallas_call(
        _unpack_kernel,
        out_shape=jax.ShapeDtypeStruct(out_shape, flat_rows.dtype),
        grid_spec=pltpu.PrefetchScalarGridSpec(
            num_scalar_prefetch=1,
            grid=(1,),
            in_specs=[_whole(flat_rows.shape)],
            out_specs=_whole(out_shape),
        ),
    )(index, flat_rows)


CTX = ("cx", "cc")


def on_device(
    input_entries, segment_entry_counts, segment_destination_part, norm_gain, kv_weight, kv_bias
):
    chips = lax.axis_size("cx")
    cores = lax.axis_size("cc")
    peer_count = chips * cores
    core = lax.axis_index("cc")
    myself = lax.axis_index("cx") * cores + core
    row_count = input_entries.shape[1]
    width = kv_weight.shape[0]
    heads_per_core = KVH // cores
    local_weight = kv_weight.reshape(width, 2, heads_per_core, cores, HD)
    local_weight = lax.dynamic_index_in_dim(local_weight, core, axis=3, keepdims=False)
    local_weight = jnp.swapaxes(local_weight, 1, 2).reshape(width, heads_per_core * 2 * HD)
    local_bias = lax.dynamic_index_in_dim(
        kv_bias.reshape(2, heads_per_core, cores, HD), core, axis=2, keepdims=False
    )
    local_bias = jnp.swapaxes(local_bias, 0, 1).reshape(-1)
    local_weight, local_bias, input_entries = lax.optimization_barrier(
        (local_weight, local_bias, input_entries)
    )
    gathered_weight = lax.all_gather(local_weight, "dp", axis=0, tiled=True)

    counts, anchors, offsets, run_ends = plan_tables(
        segment_entry_counts[0], segment_destination_part[0], peer_count
    )
    positions = jnp.arange(row_count, dtype=jnp.int32)
    capacity = 2 * row_count // peer_count
    starts = window_starts(anchors, row_count, capacity)
    lanes = 128
    width = input_entries.shape[2]
    row_blocks = input_entries[0].reshape(row_count, width // lanes, lanes)
    outgoing = pack_document_runs(row_blocks, starts[myself], peer_count, capacity)
    arriving_rows = lax.all_to_all(outgoing, CTX, split_axis=0, concat_axis=0, tiled=True)
    source, within, anchor = source_of(
        positions, run_ends[:, myself], offsets[:, myself], anchors[:, myself], peer_count
    )
    shift = anchor - jnp.take(starts[:, myself], source, mode="clip")
    index = source * capacity + shift + within
    moved_rows = unpack_runs(
        arriving_rows.reshape((peer_count * capacity,) + row_blocks.shape[1:]), index, row_count
    ).reshape(row_count, width)
    normed = rms_normed(moved_rows, norm_gain)
    sibling_rows = lax.ppermute(normed, "cc", perm=[(0, 1), (1, 0)])

    def project(rows):
        products = jnp.dot(rows, gathered_weight, preferred_element_type=jnp.float32)
        products = (products + local_bias[None, :]).astype(jnp.bfloat16)
        return jnp.swapaxes(products.reshape(row_count, heads_per_core, 2 * HD), 0, 1)

    own = project(normed)
    other = project(sibling_rows)
    first = jnp.where(core == 0, own, other)
    second = jnp.where(core == 0, other, own)
    mapped = jnp.concatenate([first, second], axis=1)
    by_heads = lax.all_to_all(mapped, "cx", split_axis=0, concat_axis=0, tiled=True)
    by_heads = by_heads.reshape(1, chips * cores * row_count, 2, 1, HD)
    return (moved_rows[None], by_heads)


def solution(mesh):
    dp_size, ctx_size = mesh.devices.shape
    cores = 2
    devices = np.asarray(mesh.devices).reshape(dp_size, ctx_size // cores, cores)
    split_mesh = Mesh(devices, ("dp", "cx", "cc"))
    in_specs = (
        P("dp", CTX, None),
        P("dp", None, None),
        P("dp", None, None),
        P(),
        P("dp", None),
        P(),
    )
    out_specs = (P("dp", CTX, None), P("dp", None, None, CTX, None))
    return jax.shard_map(
        on_device, mesh=split_mesh, in_specs=in_specs, out_specs=out_specs, check_vma=False
    )
```

```python
import jax
import jax.numpy as jnp
import numpy as np
from jax import lax
from jax.experimental import pallas as pl
from jax.experimental.pallas import tpu as pltpu
from jax.sharding import Mesh, PartitionSpec as P

KVH = 8
HD = 128


def plan_tables(lengths, targets, peer_count):
    labels = jnp.arange(peer_count, dtype=jnp.int32)
    starts = jnp.cumsum(lengths, axis=1) - lengths
    matches = (targets[:, :, None] == labels[None, None, :]).astype(jnp.int32)
    counts = jnp.sum(lengths[:, :, None] * matches, axis=1)
    anchors = jnp.sum(starts[:, :, None] * matches, axis=1)
    run_ends = jnp.cumsum(counts, axis=0)
    offsets = run_ends - counts
    return (counts, anchors, offsets, run_ends)


def source_of(positions, ends_column, offsets_column, anchors_column, peer_count):
    labels = jnp.arange(peer_count, dtype=jnp.int32)
    source = jnp.sum((ends_column[None, :] <= positions[:, None]).astype(jnp.int32), axis=1)
    chosen = (source[:, None] == labels[None, :]).astype(jnp.int32)
    within = positions - jnp.sum(chosen * offsets_column[None, :], axis=1)
    anchor = jnp.sum(chosen * anchors_column[None, :], axis=1)
    return (source, within, anchor)


def rms_normed(rows, norm_gain):
    as_float = rows.astype(jnp.float32)
    inverse_rms = lax.rsqrt(jnp.mean(as_float * as_float, axis=-1, keepdims=True) + 1e-06)
    return (as_float * inverse_rms * norm_gain[None, :]).astype(jnp.bfloat16)


def window_starts(anchors, row_count, capacity):
    return jnp.minimum(anchors, row_count - capacity)


def _pack_kernel(starts_ref, rows_ref, out_ref):
    peer_count, capacity = out_ref.shape[0], out_ref.shape[1]
    for k in range(peer_count):
        out_ref[k] = rows_ref[pl.ds(starts_ref[k], capacity)]


def _whole(shape):
    return pl.BlockSpec(shape, lambda i, *_: (0,) * len(shape))


def pack_document_runs(rows, starts, peer_count, capacity):
    out_shape = (peer_count, capacity) + rows.shape[1:]
    return pl.pallas_call(
        _pack_kernel,
        out_shape=jax.ShapeDtypeStruct(out_shape, rows.dtype),
        grid_spec=pltpu.PrefetchScalarGridSpec(
            num_scalar_prefetch=1,
            grid=(1,),
            in_specs=[_whole(rows.shape)],
            out_specs=_whole(out_shape),
        ),
    )(starts, rows)


def _unpack_kernel(index_ref, flat_ref, out_ref):
    def move_row(p, carry):
        out_ref[p] = flat_ref[index_ref[p]]
        return carry

    lax.fori_loop(0, out_ref.shape[0], move_row, 0, unroll=8)


def unpack_runs(flat_rows, index, row_count):
    out_shape = (row_count,) + flat_rows.shape[1:]
    return pl.pallas_call(
        _unpack_kernel,
        out_shape=jax.ShapeDtypeStruct(out_shape, flat_rows.dtype),
        grid_spec=pltpu.PrefetchScalarGridSpec(
            num_scalar_prefetch=1,
            grid=(1,),
            in_specs=[_whole(flat_rows.shape)],
            out_specs=_whole(out_shape),
        ),
    )(index, flat_rows)


def select_rows(rows, index):
    picks = (index[:, None] == jnp.arange(rows.shape[0], dtype=index.dtype)[None, :])
    return jnp.dot(
        picks.astype(rows.dtype), rows, preferred_element_type=jnp.float32
    ).astype(rows.dtype)


CTX = ("cx", "cc")


def on_device(
    input_entries, segment_entry_counts, segment_destination_part, norm_gain, kv_weight, kv_bias
):
    chips = lax.axis_size("cx")
    cores = lax.axis_size("cc")
    peer_count = chips * cores
    core = lax.axis_index("cc")
    myself = lax.axis_index("cx") * cores + core
    row_count = input_entries.shape[1]
    width = kv_weight.shape[0]
    heads_per_core = KVH // cores
    local_weight = kv_weight.reshape(width, 2, heads_per_core, cores, HD)
    local_weight = lax.dynamic_index_in_dim(local_weight, core, axis=3, keepdims=False)
    local_weight = jnp.swapaxes(local_weight, 1, 2).reshape(width, heads_per_core * 2 * HD)
    local_bias = lax.dynamic_index_in_dim(
        kv_bias.reshape(2, heads_per_core, cores, HD), core, axis=2, keepdims=False
    )
    local_bias = jnp.swapaxes(local_bias, 0, 1).reshape(-1)
    local_weight, local_bias, input_entries = lax.optimization_barrier(
        (local_weight, local_bias, input_entries)
    )
    gathered_weight = lax.all_gather(local_weight, "dp", axis=0, tiled=True)

    counts, anchors, offsets, run_ends = plan_tables(
        segment_entry_counts[0], segment_destination_part[0], peer_count
    )
    positions = jnp.arange(row_count, dtype=jnp.int32)
    capacity = 2 * row_count // peer_count
    starts = window_starts(anchors, row_count, capacity)
    rows = input_entries[0]
    outgoing = select_rows(rows, (starts[myself][:, None] + jnp.arange(capacity)).reshape(-1))
    arriving_rows = lax.all_to_all(
        outgoing.reshape(peer_count, capacity, -1), CTX, split_axis=0, concat_axis=0, tiled=True
    )
    source, within, anchor = source_of(
        positions, run_ends[:, myself], offsets[:, myself], anchors[:, myself], peer_count
    )
    shift = anchor - jnp.take(starts[:, myself], source, mode="clip")
    index = source * capacity + shift + within
    moved_rows = select_rows(arriving_rows.reshape(peer_count * capacity, -1), index)
    normed = rms_normed(moved_rows, norm_gain)
    sibling_rows = lax.ppermute(normed, "cc", perm=[(0, 1), (1, 0)])

    def project(rows):
        products = jnp.dot(rows, gathered_weight, preferred_element_type=jnp.float32)
        products = (products + local_bias[None, :]).astype(jnp.bfloat16)
        return jnp.swapaxes(products.reshape(row_count, heads_per_core, 2 * HD), 0, 1)

    own = project(normed)
    other = project(sibling_rows)
    first = jnp.where(core == 0, own, other)
    second = jnp.where(core == 0, other, own)
    mapped = jnp.concatenate([first, second], axis=1)
    by_heads = lax.all_to_all(mapped, "cx", split_axis=0, concat_axis=0, tiled=True)
    by_heads = by_heads.reshape(1, chips * cores * row_count, 2, 1, HD)
    return (moved_rows[None], by_heads)


def solution(mesh):
    dp_size, ctx_size = mesh.devices.shape
    cores = 2
    devices = np.asarray(mesh.devices).reshape(dp_size, ctx_size // cores, cores)
    split_mesh = Mesh(devices, ("dp", "cx", "cc"))
    in_specs = (
        P("dp", CTX, None),
        P("dp", None, None),
        P("dp", None, None),
        P(),
        P("dp", None),
        P(),
    )
    out_specs = (P("dp", CTX, None), P("dp", None, None, CTX, None))
    return jax.shard_map(
        on_device, mesh=split_mesh, in_specs=in_specs, out_specs=out_specs, check_vma=False
    )
```

```python
import jax
import jax.numpy as jnp
import numpy as np
from jax import lax
from jax.experimental import pallas as pl
from jax.experimental.pallas import tpu as pltpu
from jax.sharding import Mesh, PartitionSpec as P

KVH = 8
HD = 128


def plan_tables(lengths, targets, peer_count):
    labels = jnp.arange(peer_count, dtype=jnp.int32)
    starts = jnp.cumsum(lengths, axis=1) - lengths
    matches = (targets[:, :, None] == labels[None, None, :]).astype(jnp.int32)
    counts = jnp.sum(lengths[:, :, None] * matches, axis=1)
    anchors = jnp.sum(starts[:, :, None] * matches, axis=1)
    run_ends = jnp.cumsum(counts, axis=0)
    offsets = run_ends - counts
    return (counts, anchors, offsets, run_ends)


def source_of(positions, ends_column, offsets_column, anchors_column, peer_count):
    labels = jnp.arange(peer_count, dtype=jnp.int32)
    source = jnp.sum((ends_column[None, :] <= positions[:, None]).astype(jnp.int32), axis=1)
    chosen = (source[:, None] == labels[None, :]).astype(jnp.int32)
    within = positions - jnp.sum(chosen * offsets_column[None, :], axis=1)
    anchor = jnp.sum(chosen * anchors_column[None, :], axis=1)
    return (source, within, anchor)


def rms_normed(rows, norm_gain):
    as_float = rows.astype(jnp.float32)
    inverse_rms = lax.rsqrt(jnp.mean(as_float * as_float, axis=-1, keepdims=True) + 1e-06)
    return (as_float * inverse_rms * norm_gain[None, :]).astype(jnp.bfloat16)


def window_starts(anchors, row_count, capacity):
    return jnp.minimum(anchors, row_count - capacity)


def _pack_kernel(starts_ref, rows_ref, out_ref):
    peer_count, capacity = out_ref.shape[0], out_ref.shape[1]
    for k in range(peer_count):
        out_ref[k] = rows_ref[pl.ds(starts_ref[k], capacity)]


def _whole(shape):
    return pl.BlockSpec(shape, lambda i, *_: (0,) * len(shape))


def pack_document_runs(rows, starts, peer_count, capacity):
    out_shape = (peer_count, capacity) + rows.shape[1:]
    return pl.pallas_call(
        _pack_kernel,
        out_shape=jax.ShapeDtypeStruct(out_shape, rows.dtype),
        grid_spec=pltpu.PrefetchScalarGridSpec(
            num_scalar_prefetch=1,
            grid=(1,),
            in_specs=[_whole(rows.shape)],
            out_specs=_whole(out_shape),
        ),
    )(starts, rows)


def _unpack_kernel(index_ref, flat_ref, out_ref):
    def move_row(p, carry):
        out_ref[p] = flat_ref[index_ref[p]]
        return carry

    lax.fori_loop(0, out_ref.shape[0], move_row, 0, unroll=8)


def unpack_runs(flat_rows, index, row_count):
    out_shape = (row_count,) + flat_rows.shape[1:]
    return pl.pallas_call(
        _unpack_kernel,
        out_shape=jax.ShapeDtypeStruct(out_shape, flat_rows.dtype),
        grid_spec=pltpu.PrefetchScalarGridSpec(
            num_scalar_prefetch=1,
            grid=(1,),
            in_specs=[_whole(flat_rows.shape)],
            out_specs=_whole(out_shape),
        ),
    )(index, flat_rows)


def select_rows(rows, index):
    picks = (index[:, None] == jnp.arange(rows.shape[0], dtype=index.dtype)[None, :])
    return jnp.dot(
        picks.astype(rows.dtype), rows, preferred_element_type=jnp.float32
    ).astype(rows.dtype)


CTX = ("cx", "cc")


def on_device(
    input_entries, segment_entry_counts, segment_destination_part, norm_gain, kv_weight, kv_bias
):
    chips = lax.axis_size("cx")
    cores = lax.axis_size("cc")
    peer_count = chips * cores
    core = lax.axis_index("cc")
    myself = lax.axis_index("cx") * cores + core
    row_count = input_entries.shape[1]
    width = kv_weight.shape[0]
    heads_per_core = KVH // cores
    local_weight = kv_weight.reshape(width, 2, heads_per_core, cores, HD)
    local_weight = lax.dynamic_index_in_dim(local_weight, core, axis=3, keepdims=False)
    local_weight = jnp.swapaxes(local_weight, 1, 2).reshape(width, heads_per_core * 2 * HD)
    local_bias = lax.dynamic_index_in_dim(
        kv_bias.reshape(2, heads_per_core, cores, HD), core, axis=2, keepdims=False
    )
    local_bias = jnp.swapaxes(local_bias, 0, 1).reshape(-1)
    local_weight, local_bias, input_entries = lax.optimization_barrier(
        (local_weight, local_bias, input_entries)
    )
    gathered_weight = lax.all_gather(local_weight, "dp", axis=0, tiled=True)

    counts, anchors, offsets, run_ends = plan_tables(
        segment_entry_counts[0], segment_destination_part[0], peer_count
    )
    positions = jnp.arange(row_count, dtype=jnp.int32)
    capacity = 2 * row_count // peer_count
    starts = window_starts(anchors, row_count, capacity)
    rows = input_entries[0]
    outgoing = select_rows(rows, (starts[myself][:, None] + jnp.arange(capacity)).reshape(-1))
    arriving_rows = lax.all_to_all(
        outgoing.reshape(peer_count, capacity, -1), CTX, split_axis=0, concat_axis=0, tiled=True
    )
    source, within, anchor = source_of(
        positions, run_ends[:, myself], offsets[:, myself], anchors[:, myself], peer_count
    )
    shift = anchor - jnp.take(starts[:, myself], source, mode="clip")
    index = source * capacity + shift + within
    moved_rows = select_rows(arriving_rows.reshape(peer_count * capacity, -1), index)
    normed = rms_normed(moved_rows, norm_gain)
    sibling_rows = lax.ppermute(normed, "cc", perm=[(0, 1), (1, 0)])

    def project(rows):
        products = jnp.dot(rows, gathered_weight, preferred_element_type=jnp.float32)
        products = (products + local_bias[None, :]).astype(jnp.bfloat16)
        return jnp.swapaxes(products.reshape(row_count, heads_per_core, 2 * HD), 0, 1)

    def exchange(blocks):
        here = lax.axis_index("cx")
        gathered = jnp.zeros_like(blocks)
        gathered = lax.dynamic_update_index_in_dim(
            gathered, lax.dynamic_index_in_dim(blocks, here, 0), here, 0
        )
        for step in range(1, chips):
            outgoing_block = lax.dynamic_index_in_dim(blocks, (here + step) % chips, 0)
            arrived = lax.ppermute(
                outgoing_block, "cx", perm=[(i, (i + step) % chips) for i in range(chips)]
            )
            gathered = lax.dynamic_update_index_in_dim(
                gathered, arrived, (here + chips - step) % chips, 0
            )
        return gathered

    own = exchange(project(normed))
    other = exchange(project(sibling_rows))
    first = jnp.where(core == 0, own, other)
    second = jnp.where(core == 0, other, own)
    by_heads = jnp.concatenate([first, second], axis=1)
    by_heads = by_heads.reshape(1, chips * cores * row_count, 2, 1, HD)
    return (moved_rows[None], by_heads)


def solution(mesh):
    dp_size, ctx_size = mesh.devices.shape
    cores = 2
    devices = np.asarray(mesh.devices).reshape(dp_size, ctx_size // cores, cores)
    split_mesh = Mesh(devices, ("dp", "cx", "cc"))
    in_specs = (
        P("dp", CTX, None),
        P("dp", None, None),
        P("dp", None, None),
        P(),
        P("dp", None),
        P(),
    )
    out_specs = (P("dp", CTX, None), P("dp", None, None, CTX, None))
    return jax.shard_map(
        on_device, mesh=split_mesh, in_specs=in_specs, out_specs=out_specs, check_vma=False
    )
```

```python
import jax
import jax.numpy as jnp
import numpy as np
from jax import lax
from jax.experimental import pallas as pl
from jax.experimental.pallas import tpu as pltpu
from jax.sharding import Mesh, PartitionSpec as P

KVH = 8
HD = 128


def plan_tables(lengths, targets, peer_count):
    labels = jnp.arange(peer_count, dtype=jnp.int32)
    starts = jnp.cumsum(lengths, axis=1) - lengths
    matches = (targets[:, :, None] == labels[None, None, :]).astype(jnp.int32)
    counts = jnp.sum(lengths[:, :, None] * matches, axis=1)
    anchors = jnp.sum(starts[:, :, None] * matches, axis=1)
    run_ends = jnp.cumsum(counts, axis=0)
    offsets = run_ends - counts
    return (counts, anchors, offsets, run_ends)


def source_of(positions, ends_column, offsets_column, anchors_column, peer_count):
    labels = jnp.arange(peer_count, dtype=jnp.int32)
    source = jnp.sum((ends_column[None, :] <= positions[:, None]).astype(jnp.int32), axis=1)
    chosen = (source[:, None] == labels[None, :]).astype(jnp.int32)
    within = positions - jnp.sum(chosen * offsets_column[None, :], axis=1)
    anchor = jnp.sum(chosen * anchors_column[None, :], axis=1)
    return (source, within, anchor)


def rms_normed(rows, norm_gain):
    as_float = rows.astype(jnp.float32)
    inverse_rms = lax.rsqrt(jnp.mean(as_float * as_float, axis=-1, keepdims=True) + 1e-06)
    return (as_float * inverse_rms * norm_gain[None, :]).astype(jnp.bfloat16)


def window_starts(anchors, row_count, capacity):
    return jnp.minimum(anchors, row_count - capacity)


def _pack_kernel(starts_ref, rows_ref, out_ref):
    peer_count, capacity = out_ref.shape[0], out_ref.shape[1]
    for k in range(peer_count):
        out_ref[k] = rows_ref[pl.ds(starts_ref[k], capacity)]


def _whole(shape):
    return pl.BlockSpec(shape, lambda i, *_: (0,) * len(shape))


def pack_document_runs(rows, starts, peer_count, capacity):
    out_shape = (peer_count, capacity) + rows.shape[1:]
    return pl.pallas_call(
        _pack_kernel,
        out_shape=jax.ShapeDtypeStruct(out_shape, rows.dtype),
        grid_spec=pltpu.PrefetchScalarGridSpec(
            num_scalar_prefetch=1,
            grid=(1,),
            in_specs=[_whole(rows.shape)],
            out_specs=_whole(out_shape),
        ),
    )(starts, rows)


def _unpack_kernel(index_ref, flat_ref, out_ref):
    def move_row(p, carry):
        out_ref[p] = flat_ref[index_ref[p]]
        return carry

    lax.fori_loop(0, out_ref.shape[0], move_row, 0, unroll=8)


def unpack_runs(flat_rows, index, row_count):
    out_shape = (row_count,) + flat_rows.shape[1:]
    return pl.pallas_call(
        _unpack_kernel,
        out_shape=jax.ShapeDtypeStruct(out_shape, flat_rows.dtype),
        grid_spec=pltpu.PrefetchScalarGridSpec(
            num_scalar_prefetch=1,
            grid=(1,),
            in_specs=[_whole(flat_rows.shape)],
            out_specs=_whole(out_shape),
        ),
    )(index, flat_rows)


def select_rows(rows, index):
    picks = (index[:, None] == jnp.arange(rows.shape[0], dtype=index.dtype)[None, :])
    return jnp.dot(
        picks.astype(rows.dtype), rows, preferred_element_type=jnp.float32
    ).astype(rows.dtype)


CTX = ("cx", "cc")


def on_device(
    input_entries, segment_entry_counts, segment_destination_part, norm_gain, kv_weight, kv_bias
):
    chips = lax.axis_size("cx")
    cores = lax.axis_size("cc")
    peer_count = chips * cores
    core = lax.axis_index("cc")
    myself = lax.axis_index("cx") * cores + core
    row_count = input_entries.shape[1]
    width = kv_weight.shape[0]
    heads_per_core = KVH // cores
    here = lax.axis_index("cx")
    local_weight = kv_weight.reshape(width, 2, heads_per_core, cores, HD)
    local_weight = lax.dynamic_index_in_dim(local_weight, core, axis=3, keepdims=False)
    local_weight = jnp.roll(jnp.swapaxes(local_weight, 1, 2), -here, axis=1)
    local_weight = local_weight.reshape(width, heads_per_core * 2 * HD)
    local_bias = lax.dynamic_index_in_dim(
        kv_bias.reshape(2, heads_per_core, cores, HD), core, axis=2, keepdims=False
    )
    local_bias = jnp.roll(jnp.swapaxes(local_bias, 0, 1), -here, axis=0).reshape(-1)
    local_weight, local_bias, input_entries = lax.optimization_barrier(
        (local_weight, local_bias, input_entries)
    )
    gathered_weight = lax.all_gather(local_weight, "dp", axis=0, tiled=True)

    counts, anchors, offsets, run_ends = plan_tables(
        segment_entry_counts[0], segment_destination_part[0], peer_count
    )
    positions = jnp.arange(row_count, dtype=jnp.int32)
    capacity = 2 * row_count // peer_count
    starts = window_starts(anchors, row_count, capacity)
    rows = input_entries[0]
    outgoing = select_rows(rows, (starts[myself][:, None] + jnp.arange(capacity)).reshape(-1))
    arriving_rows = lax.all_to_all(
        outgoing.reshape(peer_count, capacity, -1), CTX, split_axis=0, concat_axis=0, tiled=True
    )
    source, within, anchor = source_of(
        positions, run_ends[:, myself], offsets[:, myself], anchors[:, myself], peer_count
    )
    shift = anchor - jnp.take(starts[:, myself], source, mode="clip")
    index = source * capacity + shift + within
    moved_rows = select_rows(arriving_rows.reshape(peer_count * capacity, -1), index)
    normed = rms_normed(moved_rows, norm_gain)
    sibling_rows = lax.ppermute(normed, "cc", perm=[(0, 1), (1, 0)])

    def project(rows):
        products = jnp.dot(rows, gathered_weight, preferred_element_type=jnp.float32)
        products = (products + local_bias[None, :]).astype(jnp.bfloat16)
        return jnp.swapaxes(products.reshape(row_count, heads_per_core, 2 * HD), 0, 1)

    own = project(normed)
    other = project(sibling_rows)
    first = jnp.where(core == 0, own, other)
    second = jnp.where(core == 0, other, own)
    mapped = jnp.concatenate([first, second], axis=1)
    by_heads = jnp.zeros_like(mapped)
    by_heads = lax.dynamic_update_index_in_dim(by_heads, mapped[0], here, 0)
    for step in range(1, chips):
        arrived = lax.ppermute(
            mapped[step], "cx", perm=[(i, (i + step) % chips) for i in range(chips)]
        )
        by_heads = lax.dynamic_update_index_in_dim(
            by_heads, arrived, (here + chips - step) % chips, 0
        )
    by_heads = by_heads.reshape(1, chips * cores * row_count, 2, 1, HD)
    return (moved_rows[None], by_heads)


def solution(mesh):
    dp_size, ctx_size = mesh.devices.shape
    cores = 2
    devices = np.asarray(mesh.devices).reshape(dp_size, ctx_size // cores, cores)
    split_mesh = Mesh(devices, ("dp", "cx", "cc"))
    in_specs = (
        P("dp", CTX, None),
        P("dp", None, None),
        P("dp", None, None),
        P(),
        P("dp", None),
        P(),
    )
    out_specs = (P("dp", CTX, None), P("dp", None, None, CTX, None))
    return jax.shard_map(
        on_device, mesh=split_mesh, in_specs=in_specs, out_specs=out_specs, check_vma=False
    )
```

```python
import jax
import jax.numpy as jnp
import numpy as np
from jax import lax
from jax.experimental import pallas as pl
from jax.experimental.pallas import tpu as pltpu
from jax.sharding import Mesh, PartitionSpec as P

KVH = 8
HD = 128


def plan_tables(lengths, targets, peer_count):
    labels = jnp.arange(peer_count, dtype=jnp.int32)
    starts = jnp.cumsum(lengths, axis=1) - lengths
    matches = (targets[:, :, None] == labels[None, None, :]).astype(jnp.int32)
    counts = jnp.sum(lengths[:, :, None] * matches, axis=1)
    anchors = jnp.sum(starts[:, :, None] * matches, axis=1)
    run_ends = jnp.cumsum(counts, axis=0)
    offsets = run_ends - counts
    return (counts, anchors, offsets, run_ends)


def source_of(positions, ends_column, offsets_column, anchors_column, peer_count):
    labels = jnp.arange(peer_count, dtype=jnp.int32)
    source = jnp.sum((ends_column[None, :] <= positions[:, None]).astype(jnp.int32), axis=1)
    chosen = (source[:, None] == labels[None, :]).astype(jnp.int32)
    within = positions - jnp.sum(chosen * offsets_column[None, :], axis=1)
    anchor = jnp.sum(chosen * anchors_column[None, :], axis=1)
    return (source, within, anchor)


def rms_normed(rows, norm_gain):
    as_float = rows.astype(jnp.float32)
    inverse_rms = lax.rsqrt(jnp.mean(as_float * as_float, axis=-1, keepdims=True) + 1e-06)
    return (as_float * inverse_rms * norm_gain[None, :]).astype(jnp.bfloat16)


def window_starts(anchors, row_count, capacity):
    return jnp.minimum(anchors, row_count - capacity)


def _pack_kernel(starts_ref, rows_ref, out_ref):
    peer_count, capacity = out_ref.shape[0], out_ref.shape[1]
    for k in range(peer_count):
        out_ref[k] = rows_ref[pl.ds(starts_ref[k], capacity)]


def _whole(shape):
    return pl.BlockSpec(shape, lambda i, *_: (0,) * len(shape))


def pack_document_runs(rows, starts, peer_count, capacity):
    out_shape = (peer_count, capacity) + rows.shape[1:]
    return pl.pallas_call(
        _pack_kernel,
        out_shape=jax.ShapeDtypeStruct(out_shape, rows.dtype),
        grid_spec=pltpu.PrefetchScalarGridSpec(
            num_scalar_prefetch=1,
            grid=(1,),
            in_specs=[_whole(rows.shape)],
            out_specs=_whole(out_shape),
        ),
    )(starts, rows)


def _unpack_kernel(index_ref, flat_ref, out_ref):
    def move_row(p, carry):
        out_ref[p] = flat_ref[index_ref[p]]
        return carry

    lax.fori_loop(0, out_ref.shape[0], move_row, 0, unroll=8)


def unpack_runs(flat_rows, index, row_count):
    out_shape = (row_count,) + flat_rows.shape[1:]
    return pl.pallas_call(
        _unpack_kernel,
        out_shape=jax.ShapeDtypeStruct(out_shape, flat_rows.dtype),
        grid_spec=pltpu.PrefetchScalarGridSpec(
            num_scalar_prefetch=1,
            grid=(1,),
            in_specs=[_whole(flat_rows.shape)],
            out_specs=_whole(out_shape),
        ),
    )(index, flat_rows)


def select_rows(rows, index):
    picks = (index[:, None] == jnp.arange(rows.shape[0], dtype=index.dtype)[None, :])
    return jnp.dot(
        picks.astype(rows.dtype), rows, preferred_element_type=jnp.float32
    ).astype(rows.dtype)


CTX = ("cx", "cc")


def on_device(
    input_entries, segment_entry_counts, segment_destination_part, norm_gain, kv_weight, kv_bias
):
    chips = lax.axis_size("cx")
    cores = lax.axis_size("cc")
    peer_count = chips * cores
    core = lax.axis_index("cc")
    myself = lax.axis_index("cx") * cores + core
    row_count = input_entries.shape[1]
    width = kv_weight.shape[0]
    heads_per_core = KVH // cores
    here = lax.axis_index("cx")
    columns = []
    for step in range(heads_per_core):
        head = ((here + step) % heads_per_core) * cores + core
        for kind in range(2):
            columns.append(kind * KVH * HD + head * HD)
    local_weight = jnp.concatenate(
        [lax.dynamic_slice_in_dim(kv_weight, c, HD, axis=1) for c in columns], axis=1
    )
    local_bias = jnp.concatenate(
        [lax.dynamic_slice_in_dim(kv_bias, c, HD, axis=0) for c in columns], axis=0
    )
    local_weight, local_bias, input_entries = lax.optimization_barrier(
        (local_weight, local_bias, input_entries)
    )
    gathered_weight = lax.all_gather(local_weight, "dp", axis=0, tiled=True)

    counts, anchors, offsets, run_ends = plan_tables(
        segment_entry_counts[0], segment_destination_part[0], peer_count
    )
    positions = jnp.arange(row_count, dtype=jnp.int32)
    capacity = 2 * row_count // peer_count
    starts = window_starts(anchors, row_count, capacity)
    rows = input_entries[0]
    outgoing = select_rows(rows, (starts[myself][:, None] + jnp.arange(capacity)).reshape(-1))
    arriving_rows = lax.all_to_all(
        outgoing.reshape(peer_count, capacity, -1), CTX, split_axis=0, concat_axis=0, tiled=True
    )
    source, within, anchor = source_of(
        positions, run_ends[:, myself], offsets[:, myself], anchors[:, myself], peer_count
    )
    shift = anchor - jnp.take(starts[:, myself], source, mode="clip")
    index = source * capacity + shift + within
    moved_rows = select_rows(arriving_rows.reshape(peer_count * capacity, -1), index)
    normed = rms_normed(moved_rows, norm_gain)
    sibling_rows = lax.ppermute(normed, "cc", perm=[(0, 1), (1, 0)])

    def project(rows):
        products = jnp.dot(rows, gathered_weight, preferred_element_type=jnp.float32)
        products = (products + local_bias[None, :]).astype(jnp.bfloat16)
        return jnp.swapaxes(products.reshape(row_count, heads_per_core, 2 * HD), 0, 1)

    own = project(normed)
    other = project(sibling_rows)
    first = jnp.where(core == 0, own, other)
    second = jnp.where(core == 0, other, own)
    mapped = jnp.concatenate([first, second], axis=1)
    by_heads = jnp.zeros_like(mapped)
    by_heads = lax.dynamic_update_index_in_dim(by_heads, mapped[0], here, 0)
    for step in range(1, chips):
        arrived = lax.ppermute(
            mapped[step], "cx", perm=[(i, (i + step) % chips) for i in range(chips)]
        )
        by_heads = lax.dynamic_update_index_in_dim(
            by_heads, arrived, (here + chips - step) % chips, 0
        )
    by_heads = by_heads.reshape(1, chips * cores * row_count, 2, 1, HD)
    return (moved_rows[None], by_heads)


def solution(mesh):
    dp_size, ctx_size = mesh.devices.shape
    cores = 2
    devices = np.asarray(mesh.devices).reshape(dp_size, ctx_size // cores, cores)
    split_mesh = Mesh(devices, ("dp", "cx", "cc"))
    in_specs = (
        P("dp", CTX, None),
        P("dp", None, None),
        P("dp", None, None),
        P(),
        P("dp", None),
        P(),
    )
    out_specs = (P("dp", CTX, None), P("dp", None, None, CTX, None))
    return jax.shard_map(
        on_device, mesh=split_mesh, in_specs=in_specs, out_specs=out_specs, check_vma=False
    )
```

```python
import jax
import jax.numpy as jnp
import numpy as np
from jax import lax
from jax.experimental import pallas as pl
from jax.experimental.pallas import tpu as pltpu
from jax.sharding import Mesh, PartitionSpec as P

KVH = 8
HD = 128


def plan_tables(lengths, targets, peer_count):
    labels = jnp.arange(peer_count, dtype=jnp.int32)
    starts = jnp.cumsum(lengths, axis=1) - lengths
    matches = (targets[:, :, None] == labels[None, None, :]).astype(jnp.int32)
    counts = jnp.sum(lengths[:, :, None] * matches, axis=1)
    anchors = jnp.sum(starts[:, :, None] * matches, axis=1)
    run_ends = jnp.cumsum(counts, axis=0)
    offsets = run_ends - counts
    return (counts, anchors, offsets, run_ends)


def source_of(positions, ends_column, offsets_column, anchors_column, peer_count):
    labels = jnp.arange(peer_count, dtype=jnp.int32)
    source = jnp.sum((ends_column[None, :] <= positions[:, None]).astype(jnp.int32), axis=1)
    chosen = (source[:, None] == labels[None, :]).astype(jnp.int32)
    within = positions - jnp.sum(chosen * offsets_column[None, :], axis=1)
    anchor = jnp.sum(chosen * anchors_column[None, :], axis=1)
    return (source, within, anchor)


def rms_normed(rows, norm_gain):
    as_float = rows.astype(jnp.float32)
    inverse_rms = lax.rsqrt(jnp.mean(as_float * as_float, axis=-1, keepdims=True) + 1e-06)
    return (as_float * inverse_rms * norm_gain[None, :]).astype(jnp.bfloat16)


def window_starts(anchors, row_count, capacity):
    return jnp.minimum(anchors, row_count - capacity)


def _pack_kernel(starts_ref, rows_ref, out_ref):
    peer_count, capacity = out_ref.shape[0], out_ref.shape[1]
    for k in range(peer_count):
        out_ref[k] = rows_ref[pl.ds(starts_ref[k], capacity)]


def _whole(shape):
    return pl.BlockSpec(shape, lambda i, *_: (0,) * len(shape))


def pack_document_runs(rows, starts, peer_count, capacity):
    out_shape = (peer_count, capacity) + rows.shape[1:]
    return pl.pallas_call(
        _pack_kernel,
        out_shape=jax.ShapeDtypeStruct(out_shape, rows.dtype),
        grid_spec=pltpu.PrefetchScalarGridSpec(
            num_scalar_prefetch=1,
            grid=(1,),
            in_specs=[_whole(rows.shape)],
            out_specs=_whole(out_shape),
        ),
    )(starts, rows)


def _unpack_kernel(index_ref, flat_ref, out_ref):
    def move_row(p, carry):
        out_ref[p] = flat_ref[index_ref[p]]
        return carry

    lax.fori_loop(0, out_ref.shape[0], move_row, 0, unroll=8)


def unpack_runs(flat_rows, index, row_count):
    out_shape = (row_count,) + flat_rows.shape[1:]
    return pl.pallas_call(
        _unpack_kernel,
        out_shape=jax.ShapeDtypeStruct(out_shape, flat_rows.dtype),
        grid_spec=pltpu.PrefetchScalarGridSpec(
            num_scalar_prefetch=1,
            grid=(1,),
            in_specs=[_whole(flat_rows.shape)],
            out_specs=_whole(out_shape),
        ),
    )(index, flat_rows)


def select_rows(rows, index):
    picks = (index[:, None] == jnp.arange(rows.shape[0], dtype=index.dtype)[None, :])
    return jnp.dot(
        picks.astype(rows.dtype), rows, preferred_element_type=jnp.float32
    ).astype(rows.dtype)


CTX = ("cx", "cc")


def on_device(
    input_entries, segment_entry_counts, segment_destination_part, norm_gain, kv_weight, kv_bias
):
    chips = lax.axis_size("cx")
    cores = lax.axis_size("cc")
    peer_count = chips * cores
    core = lax.axis_index("cc")
    myself = lax.axis_index("cx") * cores + core
    row_count = input_entries.shape[1]
    width = kv_weight.shape[0]
    heads_per_core = KVH // cores
    here = lax.axis_index("cx")

    def pick_columns(table, parity):
        starts = [
            kind * KVH * HD + (block * cores + parity) * HD
            for block in range(heads_per_core)
            for kind in range(2)
        ]
        return jnp.concatenate([table[..., c:c + HD] for c in starts], axis=-1)

    local_weight = jnp.where(core == 0, pick_columns(kv_weight, 0), pick_columns(kv_weight, 1))
    local_bias = jnp.where(core == 0, pick_columns(kv_bias, 0), pick_columns(kv_bias, 1))
    local_weight, local_bias, input_entries = lax.optimization_barrier(
        (local_weight, local_bias, input_entries)
    )
    gathered_weight = lax.all_gather(local_weight, "dp", axis=0, tiled=True)

    counts, anchors, offsets, run_ends = plan_tables(
        segment_entry_counts[0], segment_destination_part[0], peer_count
    )
    positions = jnp.arange(row_count, dtype=jnp.int32)
    capacity = 2 * row_count // peer_count
    starts = window_starts(anchors, row_count, capacity)
    rows = input_entries[0]
    outgoing = select_rows(rows, (starts[myself][:, None] + jnp.arange(capacity)).reshape(-1))
    arriving_rows = lax.all_to_all(
        outgoing.reshape(peer_count, capacity, -1), CTX, split_axis=0, concat_axis=0, tiled=True
    )
    source, within, anchor = source_of(
        positions, run_ends[:, myself], offsets[:, myself], anchors[:, myself], peer_count
    )
    shift = anchor - jnp.take(starts[:, myself], source, mode="clip")
    index = source * capacity + shift + within
    moved_rows = select_rows(arriving_rows.reshape(peer_count * capacity, -1), index)
    normed = rms_normed(moved_rows, norm_gain)
    sibling_rows = lax.ppermute(normed, "cc", perm=[(0, 1), (1, 0)])

    def project(rows):
        products = jnp.dot(rows, gathered_weight, preferred_element_type=jnp.float32)
        products = (products + local_bias[None, :]).astype(jnp.bfloat16)
        return jnp.swapaxes(products.reshape(row_count, heads_per_core, 2 * HD), 0, 1)

    own = project(normed)
    other = project(sibling_rows)
    first = jnp.where(core == 0, own, other)
    second = jnp.where(core == 0, other, own)
    mapped = jnp.roll(jnp.concatenate([first, second], axis=1), -here, axis=0)
    by_heads = jnp.zeros_like(mapped)
    by_heads = lax.dynamic_update_index_in_dim(by_heads, mapped[0], here, 0)
    for step in range(1, chips):
        arrived = lax.ppermute(
            mapped[step], "cx", perm=[(i, (i + step) % chips) for i in range(chips)]
        )
        by_heads = lax.dynamic_update_index_in_dim(
            by_heads, arrived, (here + chips - step) % chips, 0
        )
    by_heads = by_heads.reshape(1, chips * cores * row_count, 2, 1, HD)
    return (moved_rows[None], by_heads)


def solution(mesh):
    dp_size, ctx_size = mesh.devices.shape
    cores = 2
    devices = np.asarray(mesh.devices).reshape(dp_size, ctx_size // cores, cores)
    split_mesh = Mesh(devices, ("dp", "cx", "cc"))
    in_specs = (
        P("dp", CTX, None),
        P("dp", None, None),
        P("dp", None, None),
        P(),
        P("dp", None),
        P(),
    )
    out_specs = (P("dp", CTX, None), P("dp", None, None, CTX, None))
    return jax.shard_map(
        on_device, mesh=split_mesh, in_specs=in_specs, out_specs=out_specs, check_vma=False
    )
```

```python
import jax
import jax.numpy as jnp
import numpy as np
from jax import lax
from jax.experimental import pallas as pl
from jax.experimental.pallas import tpu as pltpu
from jax.experimental.layout import Layout, with_layout_constraint
from jax.sharding import Mesh, PartitionSpec as P

KVH = 8
HD = 128


def plan_tables(lengths, targets, peer_count):
    labels = jnp.arange(peer_count, dtype=jnp.int32)
    starts = jnp.cumsum(lengths, axis=1) - lengths
    matches = (targets[:, :, None] == labels[None, None, :]).astype(jnp.int32)
    counts = jnp.sum(lengths[:, :, None] * matches, axis=1)
    anchors = jnp.sum(starts[:, :, None] * matches, axis=1)
    run_ends = jnp.cumsum(counts, axis=0)
    offsets = run_ends - counts
    return (counts, anchors, offsets, run_ends)


def source_of(positions, ends_column, offsets_column, anchors_column, peer_count):
    labels = jnp.arange(peer_count, dtype=jnp.int32)
    source = jnp.sum((ends_column[None, :] <= positions[:, None]).astype(jnp.int32), axis=1)
    chosen = (source[:, None] == labels[None, :]).astype(jnp.int32)
    within = positions - jnp.sum(chosen * offsets_column[None, :], axis=1)
    anchor = jnp.sum(chosen * anchors_column[None, :], axis=1)
    return (source, within, anchor)


def rms_normed(rows, norm_gain):
    as_float = rows.astype(jnp.float32)
    inverse_rms = lax.rsqrt(jnp.mean(as_float * as_float, axis=-1, keepdims=True) + 1e-06)
    return (as_float * inverse_rms * norm_gain[None, :]).astype(jnp.bfloat16)


def window_starts(anchors, row_count, capacity):
    return jnp.minimum(anchors, row_count - capacity)


def _pack_kernel(starts_ref, rows_ref, out_ref):
    peer_count, capacity = out_ref.shape[0], out_ref.shape[1]
    for k in range(peer_count):
        out_ref[k] = rows_ref[pl.ds(starts_ref[k], capacity)]


def _whole(shape):
    return pl.BlockSpec(shape, lambda i, *_: (0,) * len(shape))


def pack_document_runs(rows, starts, peer_count, capacity):
    out_shape = (peer_count, capacity) + rows.shape[1:]
    return pl.pallas_call(
        _pack_kernel,
        out_shape=jax.ShapeDtypeStruct(out_shape, rows.dtype),
        grid_spec=pltpu.PrefetchScalarGridSpec(
            num_scalar_prefetch=1,
            grid=(1,),
            in_specs=[_whole(rows.shape)],
            out_specs=_whole(out_shape),
        ),
    )(starts, rows)


def _unpack_kernel(index_ref, flat_ref, out_ref):
    def move_row(p, carry):
        out_ref[p] = flat_ref[index_ref[p]]
        return carry

    lax.fori_loop(0, out_ref.shape[0], move_row, 0, unroll=8)


def unpack_runs(flat_rows, index, row_count):
    out_shape = (row_count,) + flat_rows.shape[1:]
    return pl.pallas_call(
        _unpack_kernel,
        out_shape=jax.ShapeDtypeStruct(out_shape, flat_rows.dtype),
        grid_spec=pltpu.PrefetchScalarGridSpec(
            num_scalar_prefetch=1,
            grid=(1,),
            in_specs=[_whole(flat_rows.shape)],
            out_specs=_whole(out_shape),
        ),
    )(index, flat_rows)


def select_rows(rows, index):
    picks = (index[:, None] == jnp.arange(rows.shape[0], dtype=index.dtype)[None, :])
    return jnp.dot(
        picks.astype(rows.dtype), rows, preferred_element_type=jnp.float32
    ).astype(rows.dtype)


CTX = ("cx", "cc")


def on_device(
    input_entries, segment_entry_counts, segment_destination_part, norm_gain, kv_weight, kv_bias
):
    chips = lax.axis_size("cx")
    cores = lax.axis_size("cc")
    peer_count = chips * cores
    core = lax.axis_index("cc")
    myself = lax.axis_index("cx") * cores + core
    row_count = input_entries.shape[1]
    width = kv_weight.shape[0]
    heads_per_core = KVH // cores
    here = lax.axis_index("cx")

    block, kind, lane = jnp.unravel_index(
        jnp.arange(heads_per_core * 2 * HD, dtype=jnp.int32), (heads_per_core, 2, HD)
    )
    head = ((here + block) % heads_per_core) * cores + core
    columns = kind * KVH * HD + head * HD + lane
    picks = jnp.arange(kv_weight.shape[1], dtype=jnp.int32)[:, None] == columns[None, :]
    local_weight = jnp.dot(
        kv_weight, picks.astype(kv_weight.dtype), preferred_element_type=jnp.float32
    ).astype(kv_weight.dtype)
    local_bias = jnp.take(kv_bias, columns, mode="clip")
    local_weight, local_bias, input_entries = lax.optimization_barrier(
        (local_weight, local_bias, input_entries)
    )
    local_weight = with_layout_constraint(local_weight, Layout(major_to_minor=(0, 1)))
    gathered_weight = lax.all_gather(local_weight, "dp", axis=0, tiled=True)
    gathered_weight = with_layout_constraint(gathered_weight, Layout(major_to_minor=(0, 1)))

    counts, anchors, offsets, run_ends = plan_tables(
        segment_entry_counts[0], segment_destination_part[0], peer_count
    )
    positions = jnp.arange(row_count, dtype=jnp.int32)
    capacity = 2 * row_count // peer_count
    starts = window_starts(anchors, row_count, capacity)
    rows = input_entries[0]
    outgoing = select_rows(rows, (starts[myself][:, None] + jnp.arange(capacity)).reshape(-1))
    arriving_rows = lax.all_to_all(
        outgoing.reshape(peer_count, capacity, -1), CTX, split_axis=0, concat_axis=0, tiled=True
    )
    source, within, anchor = source_of(
        positions, run_ends[:, myself], offsets[:, myself], anchors[:, myself], peer_count
    )
    shift = anchor - jnp.take(starts[:, myself], source, mode="clip")
    index = source * capacity + shift + within
    moved_rows = select_rows(arriving_rows.reshape(peer_count * capacity, -1), index)
    normed = rms_normed(moved_rows, norm_gain)
    sibling_rows = lax.ppermute(normed, "cc", perm=[(0, 1), (1, 0)])

    def project(rows):
        products = jnp.dot(rows, gathered_weight, preferred_element_type=jnp.float32)
        products = (products + local_bias[None, :]).astype(jnp.bfloat16)
        return jnp.swapaxes(products.reshape(row_count, heads_per_core, 2 * HD), 0, 1)

    own = project(normed)
    other = project(sibling_rows)
    first = jnp.where(core == 0, own, other)
    second = jnp.where(core == 0, other, own)
    mapped = jnp.concatenate([first, second], axis=1)
    by_heads = jnp.zeros_like(mapped)
    by_heads = lax.dynamic_update_index_in_dim(by_heads, mapped[0], here, 0)
    for step in range(1, chips):
        arrived = lax.ppermute(
            mapped[step], "cx", perm=[(i, (i + step) % chips) for i in range(chips)]
        )
        by_heads = lax.dynamic_update_index_in_dim(
            by_heads, arrived, (here + chips - step) % chips, 0
        )
    by_heads = by_heads.reshape(1, chips * cores * row_count, 2, 1, HD)
    return (moved_rows[None], by_heads)


def solution(mesh):
    dp_size, ctx_size = mesh.devices.shape
    cores = 2
    devices = np.asarray(mesh.devices).reshape(dp_size, ctx_size // cores, cores)
    split_mesh = Mesh(devices, ("dp", "cx", "cc"))
    in_specs = (
        P("dp", CTX, None),
        P("dp", None, None),
        P("dp", None, None),
        P(),
        P("dp", None),
        P(),
    )
    out_specs = (P("dp", CTX, None), P("dp", None, None, CTX, None))
    return jax.shard_map(
        on_device, mesh=split_mesh, in_specs=in_specs, out_specs=out_specs, check_vma=False
    )
```

```python
import jax
import jax.numpy as jnp
import numpy as np
from jax import lax
from jax.experimental import pallas as pl
from jax.experimental.pallas import tpu as pltpu
from jax.experimental.layout import Layout, with_layout_constraint
from jax.sharding import Mesh, PartitionSpec as P

KVH = 8
HD = 128


def plan_tables(lengths, targets, peer_count):
    labels = jnp.arange(peer_count, dtype=jnp.int32)
    starts = jnp.cumsum(lengths, axis=1) - lengths
    matches = (targets[:, :, None] == labels[None, None, :]).astype(jnp.int32)
    counts = jnp.sum(lengths[:, :, None] * matches, axis=1)
    anchors = jnp.sum(starts[:, :, None] * matches, axis=1)
    run_ends = jnp.cumsum(counts, axis=0)
    offsets = run_ends - counts
    return (counts, anchors, offsets, run_ends)


def source_of(positions, ends_column, offsets_column, anchors_column, peer_count):
    labels = jnp.arange(peer_count, dtype=jnp.int32)
    source = jnp.sum((ends_column[None, :] <= positions[:, None]).astype(jnp.int32), axis=1)
    chosen = (source[:, None] == labels[None, :]).astype(jnp.int32)
    within = positions - jnp.sum(chosen * offsets_column[None, :], axis=1)
    anchor = jnp.sum(chosen * anchors_column[None, :], axis=1)
    return (source, within, anchor)


def rms_normed(rows, norm_gain):
    as_float = rows.astype(jnp.float32)
    inverse_rms = lax.rsqrt(jnp.mean(as_float * as_float, axis=-1, keepdims=True) + 1e-06)
    return (as_float * inverse_rms * norm_gain[None, :]).astype(jnp.bfloat16)


def window_starts(anchors, row_count, capacity):
    return jnp.minimum(anchors, row_count - capacity)


def _pack_kernel(starts_ref, rows_ref, out_ref):
    peer_count, capacity = out_ref.shape[0], out_ref.shape[1]
    for k in range(peer_count):
        out_ref[k] = rows_ref[pl.ds(starts_ref[k], capacity)]


def _whole(shape):
    return pl.BlockSpec(shape, lambda i, *_: (0,) * len(shape))


def pack_document_runs(rows, starts, peer_count, capacity):
    out_shape = (peer_count, capacity) + rows.shape[1:]
    return pl.pallas_call(
        _pack_kernel,
        out_shape=jax.ShapeDtypeStruct(out_shape, rows.dtype),
        grid_spec=pltpu.PrefetchScalarGridSpec(
            num_scalar_prefetch=1,
            grid=(1,),
            in_specs=[_whole(rows.shape)],
            out_specs=_whole(out_shape),
        ),
    )(starts, rows)


def _unpack_kernel(index_ref, flat_ref, out_ref):
    def move_row(p, carry):
        out_ref[p] = flat_ref[index_ref[p]]
        return carry

    lax.fori_loop(0, out_ref.shape[0], move_row, 0, unroll=8)


def unpack_runs(flat_rows, index, row_count):
    out_shape = (row_count,) + flat_rows.shape[1:]
    return pl.pallas_call(
        _unpack_kernel,
        out_shape=jax.ShapeDtypeStruct(out_shape, flat_rows.dtype),
        grid_spec=pltpu.PrefetchScalarGridSpec(
            num_scalar_prefetch=1,
            grid=(1,),
            in_specs=[_whole(flat_rows.shape)],
            out_specs=_whole(out_shape),
        ),
    )(index, flat_rows)


def select_rows(rows, index):
    picks = (index[:, None] == jnp.arange(rows.shape[0], dtype=index.dtype)[None, :])
    return jnp.dot(
        picks.astype(rows.dtype), rows, preferred_element_type=jnp.float32
    ).astype(rows.dtype)


CTX = ("cx", "cc")


def on_device(
    input_entries, segment_entry_counts, segment_destination_part, norm_gain, kv_weight, kv_bias
):
    chips = lax.axis_size("cx")
    cores = lax.axis_size("cc")
    peer_count = chips * cores
    core = lax.axis_index("cc")
    myself = lax.axis_index("cx") * cores + core
    row_count = input_entries.shape[1]
    width = kv_weight.shape[0]
    heads_per_core = KVH // cores
    here = lax.axis_index("cx")

    block, kind, lane = jnp.unravel_index(
        jnp.arange(heads_per_core * 2 * HD, dtype=jnp.int32), (heads_per_core, 2, HD)
    )
    head = ((here + block) % heads_per_core) * cores + core
    columns = kind * KVH * HD + head * HD + lane
    picks = jnp.arange(kv_weight.shape[1], dtype=jnp.int32)[:, None] == columns[None, :]
    local_weight = jnp.dot(
        kv_weight, picks.astype(kv_weight.dtype), preferred_element_type=jnp.float32
    ).astype(kv_weight.dtype)
    local_bias = jnp.take(kv_bias, columns, mode="clip")
    local_weight, input_entries = lax.optimization_barrier((local_weight, input_entries))
    local_weight = with_layout_constraint(local_weight, Layout(major_to_minor=(0, 1)))
    gathered_weight = lax.all_gather(local_weight, "dp", axis=0, tiled=True)
    gathered_weight = with_layout_constraint(gathered_weight, Layout(major_to_minor=(0, 1)))

    counts, anchors, offsets, run_ends = plan_tables(
        segment_entry_counts[0], segment_destination_part[0], peer_count
    )
    positions = jnp.arange(row_count, dtype=jnp.int32)
    capacity = 2 * row_count // peer_count
    starts = window_starts(anchors, row_count, capacity)
    rows = input_entries[0]
    outgoing = select_rows(rows, (starts[myself][:, None] + jnp.arange(capacity)).reshape(-1))
    arriving_rows = lax.all_to_all(
        outgoing.reshape(peer_count, capacity, -1), CTX, split_axis=0, concat_axis=0, tiled=True
    )
    source, within, anchor = source_of(
        positions, run_ends[:, myself], offsets[:, myself], anchors[:, myself], peer_count
    )
    shift = anchor - jnp.take(starts[:, myself], source, mode="clip")
    index = source * capacity + shift + within
    moved_rows = select_rows(arriving_rows.reshape(peer_count * capacity, -1), index)
    normed = rms_normed(moved_rows, norm_gain)
    sibling_rows = lax.ppermute(normed, "cc", perm=[(0, 1), (1, 0)])

    def project(rows):
        products = jnp.dot(rows, gathered_weight, preferred_element_type=jnp.float32)
        products = (products + local_bias[None, :]).astype(jnp.bfloat16)
        return jnp.swapaxes(products.reshape(row_count, heads_per_core, 2 * HD), 0, 1)

    own = project(normed)
    other = project(sibling_rows)
    first = jnp.where(core == 0, own, other)
    second = jnp.where(core == 0, other, own)
    mapped = jnp.concatenate([first, second], axis=1)
    by_heads = jnp.zeros_like(mapped)
    by_heads = lax.dynamic_update_index_in_dim(by_heads, mapped[0], here, 0)
    for step in range(1, chips):
        arrived = lax.ppermute(
            mapped[step], "cx", perm=[(i, (i + step) % chips) for i in range(chips)]
        )
        by_heads = lax.dynamic_update_index_in_dim(
            by_heads, arrived, (here + chips - step) % chips, 0
        )
    by_heads = by_heads.reshape(1, chips * cores * row_count, 2, 1, HD)
    return (moved_rows[None], by_heads)


def solution(mesh):
    dp_size, ctx_size = mesh.devices.shape
    cores = 2
    devices = np.asarray(mesh.devices).reshape(dp_size, ctx_size // cores, cores)
    split_mesh = Mesh(devices, ("dp", "cx", "cc"))
    in_specs = (
        P("dp", CTX, None),
        P("dp", None, None),
        P("dp", None, None),
        P(),
        P("dp", None),
        P(),
    )
    out_specs = (P("dp", CTX, None), P("dp", None, None, CTX, None))
    return jax.shard_map(
        on_device, mesh=split_mesh, in_specs=in_specs, out_specs=out_specs, check_vma=False
    )
```

```python
import jax
import jax.numpy as jnp
import numpy as np
from jax import lax
from jax.experimental import pallas as pl
from jax.experimental.pallas import tpu as pltpu
from jax.experimental.layout import Layout, with_layout_constraint
from jax.sharding import Mesh, PartitionSpec as P

KVH = 8
HD = 128


def plan_tables(lengths, targets, peer_count):
    labels = jnp.arange(peer_count, dtype=jnp.int32)
    starts = jnp.cumsum(lengths, axis=1) - lengths
    matches = (targets[:, :, None] == labels[None, None, :]).astype(jnp.int32)
    counts = jnp.sum(lengths[:, :, None] * matches, axis=1)
    anchors = jnp.sum(starts[:, :, None] * matches, axis=1)
    run_ends = jnp.cumsum(counts, axis=0)
    offsets = run_ends - counts
    return (counts, anchors, offsets, run_ends)


def source_of(positions, ends_column, offsets_column, anchors_column, peer_count):
    labels = jnp.arange(peer_count, dtype=jnp.int32)
    source = jnp.sum((ends_column[None, :] <= positions[:, None]).astype(jnp.int32), axis=1)
    chosen = (source[:, None] == labels[None, :]).astype(jnp.int32)
    within = positions - jnp.sum(chosen * offsets_column[None, :], axis=1)
    anchor = jnp.sum(chosen * anchors_column[None, :], axis=1)
    return (source, within, anchor)


def rms_normed(rows, norm_gain):
    as_float = rows.astype(jnp.float32)
    inverse_rms = lax.rsqrt(jnp.mean(as_float * as_float, axis=-1, keepdims=True) + 1e-06)
    return (as_float * inverse_rms * norm_gain[None, :]).astype(jnp.bfloat16)


def window_starts(anchors, row_count, capacity):
    return jnp.minimum(anchors, row_count - capacity)


def _pack_kernel(starts_ref, rows_ref, out_ref):
    peer_count, capacity = out_ref.shape[0], out_ref.shape[1]
    for k in range(peer_count):
        out_ref[k] = rows_ref[pl.ds(starts_ref[k], capacity)]


def _whole(shape):
    return pl.BlockSpec(shape, lambda i, *_: (0,) * len(shape))


def pack_document_runs(rows, starts, peer_count, capacity):
    out_shape = (peer_count, capacity) + rows.shape[1:]
    return pl.pallas_call(
        _pack_kernel,
        out_shape=jax.ShapeDtypeStruct(out_shape, rows.dtype),
        grid_spec=pltpu.PrefetchScalarGridSpec(
            num_scalar_prefetch=1,
            grid=(1,),
            in_specs=[_whole(rows.shape)],
            out_specs=_whole(out_shape),
        ),
    )(starts, rows)


def _unpack_kernel(index_ref, flat_ref, out_ref):
    def move_row(p, carry):
        out_ref[p] = flat_ref[index_ref[p]]
        return carry

    lax.fori_loop(0, out_ref.shape[0], move_row, 0, unroll=8)


def unpack_runs(flat_rows, index, row_count):
    out_shape = (row_count,) + flat_rows.shape[1:]
    return pl.pallas_call(
        _unpack_kernel,
        out_shape=jax.ShapeDtypeStruct(out_shape, flat_rows.dtype),
        grid_spec=pltpu.PrefetchScalarGridSpec(
            num_scalar_prefetch=1,
            grid=(1,),
            in_specs=[_whole(flat_rows.shape)],
            out_specs=_whole(out_shape),
        ),
    )(index, flat_rows)


def select_rows(rows, index):
    picks = (index[:, None] == jnp.arange(rows.shape[0], dtype=index.dtype)[None, :])
    return jnp.dot(
        picks.astype(rows.dtype), rows, preferred_element_type=jnp.float32
    ).astype(rows.dtype)


CTX = ("cx", "cc")


def on_device(
    input_entries, segment_entry_counts, segment_destination_part, norm_gain, kv_weight, kv_bias
):
    chips = lax.axis_size("cx")
    cores = lax.axis_size("cc")
    peer_count = chips * cores
    core = lax.axis_index("cc")
    myself = lax.axis_index("cx") * cores + core
    row_count = input_entries.shape[1]
    width = kv_weight.shape[0]
    heads_per_core = KVH // cores
    here = lax.axis_index("cx")

    block, kind, lane = jnp.unravel_index(
        jnp.arange(heads_per_core * 2 * HD, dtype=jnp.int32), (heads_per_core, 2, HD)
    )
    head = ((here + block) % heads_per_core) * cores + core
    columns = kind * KVH * HD + head * HD + lane
    picks = jnp.arange(kv_weight.shape[1], dtype=jnp.int32)[:, None] == columns[None, :]
    local_weight = jnp.dot(
        kv_weight, picks.astype(kv_weight.dtype), preferred_element_type=jnp.float32
    ).astype(kv_weight.dtype)
    local_bias = jnp.take(kv_bias, columns, mode="clip")
    local_weight, input_entries = lax.optimization_barrier((local_weight, input_entries))
    local_weight = with_layout_constraint(local_weight, Layout(major_to_minor=(0, 1)))
    gathered_weight = lax.all_gather(local_weight, "dp", axis=0, tiled=True)
    gathered_weight = with_layout_constraint(gathered_weight, Layout(major_to_minor=(0, 1)))

    counts, anchors, offsets, run_ends = plan_tables(
        segment_entry_counts[0], segment_destination_part[0], peer_count
    )
    positions = jnp.arange(row_count, dtype=jnp.int32)
    capacity = 2 * row_count // peer_count
    starts = window_starts(anchors, row_count, capacity)
    rows = input_entries[0]
    outgoing = select_rows(rows, (starts[myself][:, None] + jnp.arange(capacity)).reshape(-1))
    arriving_rows = lax.all_to_all(
        outgoing.reshape(peer_count, capacity, -1), CTX, split_axis=0, concat_axis=0, tiled=True
    )
    source, within, anchor = source_of(
        positions, run_ends[:, myself], offsets[:, myself], anchors[:, myself], peer_count
    )
    shift = anchor - jnp.take(starts[:, myself], source, mode="clip")
    index = source * capacity + shift + within
    local_bias, index = lax.optimization_barrier((local_bias, index))
    moved_rows = select_rows(arriving_rows.reshape(peer_count * capacity, -1), index)
    normed = rms_normed(moved_rows, norm_gain)
    sibling_rows = lax.ppermute(normed, "cc", perm=[(0, 1), (1, 0)])

    def project(rows):
        products = jnp.dot(rows, gathered_weight, preferred_element_type=jnp.float32)
        products = (products + local_bias[None, :]).astype(jnp.bfloat16)
        return jnp.swapaxes(products.reshape(row_count, heads_per_core, 2 * HD), 0, 1)

    own = project(normed)
    other = project(sibling_rows)
    first = jnp.where(core == 0, own, other)
    second = jnp.where(core == 0, other, own)
    mapped = jnp.concatenate([first, second], axis=1)
    by_heads = jnp.zeros_like(mapped)
    by_heads = lax.dynamic_update_index_in_dim(by_heads, mapped[0], here, 0)
    for step in range(1, chips):
        arrived = lax.ppermute(
            mapped[step], "cx", perm=[(i, (i + step) % chips) for i in range(chips)]
        )
        by_heads = lax.dynamic_update_index_in_dim(
            by_heads, arrived, (here + chips - step) % chips, 0
        )
    by_heads = by_heads.reshape(1, chips * cores * row_count, 2, 1, HD)
    return (moved_rows[None], by_heads)


def solution(mesh):
    dp_size, ctx_size = mesh.devices.shape
    cores = 2
    devices = np.asarray(mesh.devices).reshape(dp_size, ctx_size // cores, cores)
    split_mesh = Mesh(devices, ("dp", "cx", "cc"))
    in_specs = (
        P("dp", CTX, None),
        P("dp", None, None),
        P("dp", None, None),
        P(),
        P("dp", None),
        P(),
    )
    out_specs = (P("dp", CTX, None), P("dp", None, None, CTX, None))
    return jax.shard_map(
        on_device, mesh=split_mesh, in_specs=in_specs, out_specs=out_specs, check_vma=False
    )
```

```python
import jax
import jax.numpy as jnp
import numpy as np
from jax import lax
from jax.experimental import pallas as pl
from jax.experimental.pallas import tpu as pltpu
from jax.experimental.layout import Layout, with_layout_constraint
from jax.sharding import Mesh, PartitionSpec as P

KVH = 8
HD = 128


def plan_tables(lengths, targets, peer_count):
    labels = jnp.arange(peer_count, dtype=jnp.int32)
    starts = jnp.cumsum(lengths, axis=1) - lengths
    matches = (targets[:, :, None] == labels[None, None, :]).astype(jnp.int32)
    counts = jnp.sum(lengths[:, :, None] * matches, axis=1)
    anchors = jnp.sum(starts[:, :, None] * matches, axis=1)
    run_ends = jnp.cumsum(counts, axis=0)
    offsets = run_ends - counts
    return (counts, anchors, offsets, run_ends)


def source_of(positions, ends_column, offsets_column, anchors_column, peer_count):
    labels = jnp.arange(peer_count, dtype=jnp.int32)
    source = jnp.sum((ends_column[None, :] <= positions[:, None]).astype(jnp.int32), axis=1)
    chosen = (source[:, None] == labels[None, :]).astype(jnp.int32)
    within = positions - jnp.sum(chosen * offsets_column[None, :], axis=1)
    anchor = jnp.sum(chosen * anchors_column[None, :], axis=1)
    return (source, within, anchor)


def rms_normed(rows, norm_gain):
    as_float = rows.astype(jnp.float32)
    inverse_rms = lax.rsqrt(jnp.mean(as_float * as_float, axis=-1, keepdims=True) + 1e-06)
    return (as_float * inverse_rms * norm_gain[None, :]).astype(jnp.bfloat16)


def window_starts(anchors, row_count, capacity):
    return jnp.minimum(anchors, row_count - capacity)


def _pack_kernel(starts_ref, rows_ref, out_ref):
    peer_count, capacity = out_ref.shape[0], out_ref.shape[1]
    for k in range(peer_count):
        out_ref[k] = rows_ref[pl.ds(starts_ref[k], capacity)]


def _whole(shape):
    return pl.BlockSpec(shape, lambda i, *_: (0,) * len(shape))


def pack_document_runs(rows, starts, peer_count, capacity):
    out_shape = (peer_count, capacity) + rows.shape[1:]
    return pl.pallas_call(
        _pack_kernel,
        out_shape=jax.ShapeDtypeStruct(out_shape, rows.dtype),
        grid_spec=pltpu.PrefetchScalarGridSpec(
            num_scalar_prefetch=1,
            grid=(1,),
            in_specs=[_whole(rows.shape)],
            out_specs=_whole(out_shape),
        ),
    )(starts, rows)


def _unpack_kernel(index_ref, flat_ref, out_ref):
    def move_row(p, carry):
        out_ref[p] = flat_ref[index_ref[p]]
        return carry

    lax.fori_loop(0, out_ref.shape[0], move_row, 0, unroll=8)


def unpack_runs(flat_rows, index, row_count):
    out_shape = (row_count,) + flat_rows.shape[1:]
    return pl.pallas_call(
        _unpack_kernel,
        out_shape=jax.ShapeDtypeStruct(out_shape, flat_rows.dtype),
        grid_spec=pltpu.PrefetchScalarGridSpec(
            num_scalar_prefetch=1,
            grid=(1,),
            in_specs=[_whole(flat_rows.shape)],
            out_specs=_whole(out_shape),
        ),
    )(index, flat_rows)


def select_rows(rows, index):
    picks = (index[:, None] == jnp.arange(rows.shape[0], dtype=index.dtype)[None, :])
    return jnp.dot(
        picks.astype(rows.dtype), rows, preferred_element_type=jnp.float32
    ).astype(rows.dtype)


CTX = ("cx", "cc")


def on_device(
    input_entries, segment_entry_counts, segment_destination_part, norm_gain, kv_weight, kv_bias
):
    chips = lax.axis_size("cx")
    cores = lax.axis_size("cc")
    peer_count = chips * cores
    core = lax.axis_index("cc")
    myself = lax.axis_index("cx") * cores + core
    row_count = input_entries.shape[1]
    width = kv_weight.shape[0]
    heads_per_core = KVH // cores
    here = lax.axis_index("cx")

    block, kind, lane = jnp.unravel_index(
        jnp.arange(heads_per_core * 2 * HD, dtype=jnp.int32), (heads_per_core, 2, HD)
    )
    head = ((here + block) % heads_per_core) * cores + core
    columns = kind * KVH * HD + head * HD + lane
    picks = jnp.arange(kv_weight.shape[1], dtype=jnp.int32)[:, None] == columns[None, :]
    local_weight = jnp.dot(
        kv_weight, picks.astype(kv_weight.dtype), preferred_element_type=jnp.float32
    ).astype(kv_weight.dtype)
    local_bias = jnp.take(kv_bias, columns, mode="clip")
    local_weight, input_entries = lax.optimization_barrier((local_weight, input_entries))
    local_weight = with_layout_constraint(local_weight, Layout(major_to_minor=(0, 1)))
    gathered_weight = lax.all_gather(local_weight, "dp", axis=0, tiled=True)
    gathered_weight = with_layout_constraint(gathered_weight, Layout(major_to_minor=(0, 1)))

    counts, anchors, offsets, run_ends = plan_tables(
        segment_entry_counts[0], segment_destination_part[0], peer_count
    )
    positions = jnp.arange(row_count, dtype=jnp.int32)
    capacity = 2 * row_count // peer_count
    starts = window_starts(anchors, row_count, capacity)
    rows = input_entries[0]
    outgoing = select_rows(rows, (starts[myself][:, None] + jnp.arange(capacity)).reshape(-1))
    arriving_rows = lax.all_to_all(
        outgoing.reshape(peer_count, capacity, -1), CTX, split_axis=0, concat_axis=0, tiled=True
    )
    source, within, anchor = source_of(
        positions, run_ends[:, myself], offsets[:, myself], anchors[:, myself], peer_count
    )
    shift = anchor - jnp.take(starts[:, myself], source, mode="clip")
    index = source * capacity + shift + within
    local_bias, index = lax.optimization_barrier((local_bias, index))
    moved_rows = select_rows(arriving_rows.reshape(peer_count * capacity, -1), index)
    gathered_weight, moved_rows = lax.optimization_barrier((gathered_weight, moved_rows))
    normed = rms_normed(moved_rows, norm_gain)
    sibling_rows = lax.ppermute(normed, "cc", perm=[(0, 1), (1, 0)])

    def project(rows):
        products = jnp.dot(rows, gathered_weight, preferred_element_type=jnp.float32)
        products = (products + local_bias[None, :]).astype(jnp.bfloat16)
        return jnp.swapaxes(products.reshape(row_count, heads_per_core, 2 * HD), 0, 1)

    own = project(normed)
    other = project(sibling_rows)
    first = jnp.where(core == 0, own, other)
    second = jnp.where(core == 0, other, own)
    mapped = jnp.concatenate([first, second], axis=1)
    by_heads = jnp.zeros_like(mapped)
    by_heads = lax.dynamic_update_index_in_dim(by_heads, mapped[0], here, 0)
    for step in range(1, chips):
        arrived = lax.ppermute(
            mapped[step], "cx", perm=[(i, (i + step) % chips) for i in range(chips)]
        )
        by_heads = lax.dynamic_update_index_in_dim(
            by_heads, arrived, (here + chips - step) % chips, 0
        )
    by_heads = by_heads.reshape(1, chips * cores * row_count, 2, 1, HD)
    return (moved_rows[None], by_heads)


def solution(mesh):
    dp_size, ctx_size = mesh.devices.shape
    cores = 2
    devices = np.asarray(mesh.devices).reshape(dp_size, ctx_size // cores, cores)
    split_mesh = Mesh(devices, ("dp", "cx", "cc"))
    in_specs = (
        P("dp", CTX, None),
        P("dp", None, None),
        P("dp", None, None),
        P(),
        P("dp", None),
        P(),
    )
    out_specs = (P("dp", CTX, None), P("dp", None, None, CTX, None))
    return jax.shard_map(
        on_device, mesh=split_mesh, in_specs=in_specs, out_specs=out_specs, check_vma=False
    )
```

```python
import jax
import jax.numpy as jnp
import numpy as np
from jax import lax
from jax.experimental import pallas as pl
from jax.experimental.pallas import tpu as pltpu
from jax.experimental.layout import Layout, with_layout_constraint
from jax.sharding import Mesh, PartitionSpec as P

KVH = 8
HD = 128


def plan_tables(lengths, targets, peer_count):
    labels = jnp.arange(peer_count, dtype=jnp.int32)
    starts = jnp.cumsum(lengths, axis=1) - lengths
    matches = (targets[:, :, None] == labels[None, None, :]).astype(jnp.int32)
    counts = jnp.sum(lengths[:, :, None] * matches, axis=1)
    anchors = jnp.sum(starts[:, :, None] * matches, axis=1)
    run_ends = jnp.cumsum(counts, axis=0)
    offsets = run_ends - counts
    return (counts, anchors, offsets, run_ends)


def source_of(positions, ends_column, offsets_column, anchors_column, peer_count):
    labels = jnp.arange(peer_count, dtype=jnp.int32)
    source = jnp.sum((ends_column[None, :] <= positions[:, None]).astype(jnp.int32), axis=1)
    chosen = (source[:, None] == labels[None, :]).astype(jnp.int32)
    within = positions - jnp.sum(chosen * offsets_column[None, :], axis=1)
    anchor = jnp.sum(chosen * anchors_column[None, :], axis=1)
    return (source, within, anchor)


def rms_normed(rows, norm_gain):
    as_float = rows.astype(jnp.float32)
    inverse_rms = lax.rsqrt(jnp.mean(as_float * as_float, axis=-1, keepdims=True) + 1e-06)
    return (as_float * inverse_rms * norm_gain[None, :]).astype(jnp.bfloat16)


def window_starts(anchors, row_count, capacity):
    return jnp.minimum(anchors, row_count - capacity)


def _pack_kernel(starts_ref, rows_ref, out_ref):
    peer_count, capacity = out_ref.shape[0], out_ref.shape[1]
    for k in range(peer_count):
        out_ref[k] = rows_ref[pl.ds(starts_ref[k], capacity)]


def _whole(shape):
    return pl.BlockSpec(shape, lambda i, *_: (0,) * len(shape))


def pack_document_runs(rows, starts, peer_count, capacity):
    out_shape = (peer_count, capacity) + rows.shape[1:]
    return pl.pallas_call(
        _pack_kernel,
        out_shape=jax.ShapeDtypeStruct(out_shape, rows.dtype),
        grid_spec=pltpu.PrefetchScalarGridSpec(
            num_scalar_prefetch=1,
            grid=(1,),
            in_specs=[_whole(rows.shape)],
            out_specs=_whole(out_shape),
        ),
    )(starts, rows)


def _unpack_kernel(index_ref, flat_ref, out_ref):
    def move_row(p, carry):
        out_ref[p] = flat_ref[index_ref[p]]
        return carry

    lax.fori_loop(0, out_ref.shape[0], move_row, 0, unroll=8)


def unpack_runs(flat_rows, index, row_count):
    out_shape = (row_count,) + flat_rows.shape[1:]
    return pl.pallas_call(
        _unpack_kernel,
        out_shape=jax.ShapeDtypeStruct(out_shape, flat_rows.dtype),
        grid_spec=pltpu.PrefetchScalarGridSpec(
            num_scalar_prefetch=1,
            grid=(1,),
            in_specs=[_whole(flat_rows.shape)],
            out_specs=_whole(out_shape),
        ),
    )(index, flat_rows)


def select_rows(rows, index):
    picks = (index[:, None] == jnp.arange(rows.shape[0], dtype=index.dtype)[None, :])
    return jnp.dot(
        picks.astype(rows.dtype), rows, preferred_element_type=jnp.float32
    ).astype(rows.dtype)


CTX = ("cx", "cc")


def on_device(
    input_entries, segment_entry_counts, segment_destination_part, norm_gain, kv_weight, kv_bias
):
    chips = lax.axis_size("cx")
    cores = lax.axis_size("cc")
    peer_count = chips * cores
    core = lax.axis_index("cc")
    myself = lax.axis_index("cx") * cores + core
    row_count = input_entries.shape[1]
    width = kv_weight.shape[0]
    heads_per_core = KVH // cores
    here = lax.axis_index("cx")

    block, kind, lane = jnp.unravel_index(
        jnp.arange(heads_per_core * 2 * HD, dtype=jnp.int32), (heads_per_core, 2, HD)
    )
    head = ((here + block) % heads_per_core) * cores + core
    columns = kind * KVH * HD + head * HD + lane
    picks = jnp.arange(kv_weight.shape[1], dtype=jnp.int32)[:, None] == columns[None, :]
    local_weight = jnp.dot(
        kv_weight, picks.astype(kv_weight.dtype), preferred_element_type=jnp.float32
    ).astype(kv_weight.dtype)
    local_bias = jnp.take(kv_bias, columns, mode="clip")
    local_weight, input_entries = lax.optimization_barrier((local_weight, input_entries))
    local_weight = with_layout_constraint(local_weight, Layout(major_to_minor=(0, 1)))
    gathered_weight = lax.all_gather(local_weight, "dp", axis=0, tiled=True)
    gathered_weight = with_layout_constraint(gathered_weight, Layout(major_to_minor=(0, 1)))

    counts, anchors, offsets, run_ends = plan_tables(
        segment_entry_counts[0], segment_destination_part[0], peer_count
    )
    positions = jnp.arange(row_count, dtype=jnp.int32)
    capacity = 2 * row_count // peer_count
    starts = window_starts(anchors, row_count, capacity)
    rows = input_entries[0]
    outgoing = select_rows(rows, (starts[myself][:, None] + jnp.arange(capacity)).reshape(-1))
    arriving_rows = lax.all_to_all(
        outgoing.reshape(peer_count, capacity, -1), CTX, split_axis=0, concat_axis=0, tiled=True
    )
    source, within, anchor = source_of(
        positions, run_ends[:, myself], offsets[:, myself], anchors[:, myself], peer_count
    )
    shift = anchor - jnp.take(starts[:, myself], source, mode="clip")
    index = source * capacity + shift + within
    local_bias, index = lax.optimization_barrier((local_bias, index))
    moved_rows = select_rows(arriving_rows.reshape(peer_count * capacity, -1), index)
    normed = rms_normed(moved_rows, norm_gain)
    sibling_rows = lax.ppermute(normed, "cc", perm=[(0, 1), (1, 0)])

    def project(rows):
        products = jnp.dot(rows, gathered_weight, preferred_element_type=jnp.float32)
        products = (products + local_bias[None, :]).astype(jnp.bfloat16)
        return jnp.swapaxes(products.reshape(row_count, heads_per_core, 2 * HD), 0, 1)

    own = project(normed)
    other = project(sibling_rows)
    first = jnp.where(core == 0, own, other)
    second = jnp.where(core == 0, other, own)
    mapped = jnp.concatenate([first, second], axis=1)
    chip_rows = cores * row_count

    def as_rows(block):
        return block.reshape(1, chip_rows, 2, 1, HD)

    by_heads = jnp.zeros((1, chips * chip_rows, 2, 1, HD), mapped.dtype)
    by_heads = lax.dynamic_update_slice_in_dim(by_heads, as_rows(mapped[0]), here * chip_rows, 1)
    for step in range(1, chips):
        arrived = lax.ppermute(
            mapped[step], "cx", perm=[(i, (i + step) % chips) for i in range(chips)]
        )
        by_heads = lax.dynamic_update_slice_in_dim(
            by_heads, as_rows(arrived), ((here + chips - step) % chips) * chip_rows, 1
        )
    return (moved_rows[None], by_heads)


def solution(mesh):
    dp_size, ctx_size = mesh.devices.shape
    cores = 2
    devices = np.asarray(mesh.devices).reshape(dp_size, ctx_size // cores, cores)
    split_mesh = Mesh(devices, ("dp", "cx", "cc"))
    in_specs = (
        P("dp", CTX, None),
        P("dp", None, None),
        P("dp", None, None),
        P(),
        P("dp", None),
        P(),
    )
    out_specs = (P("dp", CTX, None), P("dp", None, None, CTX, None))
    return jax.shard_map(
        on_device, mesh=split_mesh, in_specs=in_specs, out_specs=out_specs, check_vma=False
    )
```

```python
import jax
import jax.numpy as jnp
import numpy as np
from jax import lax
from jax.experimental import pallas as pl
from jax.experimental.pallas import tpu as pltpu
from jax.experimental.layout import Layout, with_layout_constraint
from jax.sharding import Mesh, PartitionSpec as P

KVH = 8
HD = 128


def plan_tables(lengths, targets, peer_count):
    labels = jnp.arange(peer_count, dtype=jnp.int32)
    starts = jnp.cumsum(lengths, axis=1) - lengths
    matches = (targets[:, :, None] == labels[None, None, :]).astype(jnp.int32)
    counts = jnp.sum(lengths[:, :, None] * matches, axis=1)
    anchors = jnp.sum(starts[:, :, None] * matches, axis=1)
    run_ends = jnp.cumsum(counts, axis=0)
    offsets = run_ends - counts
    return (counts, anchors, offsets, run_ends)


def source_of(positions, ends_column, offsets_column, anchors_column, peer_count):
    labels = jnp.arange(peer_count, dtype=jnp.int32)
    source = jnp.sum((ends_column[None, :] <= positions[:, None]).astype(jnp.int32), axis=1)
    chosen = (source[:, None] == labels[None, :]).astype(jnp.int32)
    within = positions - jnp.sum(chosen * offsets_column[None, :], axis=1)
    anchor = jnp.sum(chosen * anchors_column[None, :], axis=1)
    return (source, within, anchor)


def rms_normed(rows, norm_gain):
    as_float = rows.astype(jnp.float32)
    inverse_rms = lax.rsqrt(jnp.mean(as_float * as_float, axis=-1, keepdims=True) + 1e-06)
    return (as_float * inverse_rms * norm_gain[None, :]).astype(jnp.bfloat16)


def window_starts(anchors, row_count, capacity):
    return jnp.minimum(anchors, row_count - capacity)


def _pack_kernel(starts_ref, rows_ref, out_ref):
    peer_count, capacity = out_ref.shape[0], out_ref.shape[1]
    for k in range(peer_count):
        out_ref[k] = rows_ref[pl.ds(starts_ref[k], capacity)]


def _exchange_kernel(blocks_ref, out_ref, landed, send_sems, recv_sems):
    chips = blocks_ref.shape[0]
    here = lax.axis_index("cx")
    barrier = pltpu.get_barrier_semaphore()
    for step in range(1, chips):
        pl.semaphore_signal(
            barrier, inc=1, device_id={"cx": (here + step) % chips},
            device_id_type=pl.DeviceIdType.MESH,
        )
    pl.semaphore_wait(barrier, chips - 1)
    copies = []
    for step in range(1, chips):
        copy = pltpu.make_async_remote_copy(
            src_ref=blocks_ref.at[step],
            dst_ref=landed.at[step - 1],
            send_sem=send_sems.at[step - 1],
            recv_sem=recv_sems.at[step - 1],
            device_id={"cx": (here + step) % chips},
            device_id_type=pl.DeviceIdType.MESH,
        )
        copy.start()
        copies.append(copy)
    out_ref[here] = blocks_ref[0]
    for step in range(1, chips):
        copies[step - 1].wait_send()
        copies[step - 1].wait_recv()
        out_ref[(here + chips - step) % chips] = landed[step - 1]


def exchange_blocks(blocks):
    chips = blocks.shape[0]
    whole = pl.BlockSpec(memory_space=pltpu.VMEM)
    return pl.pallas_call(
        _exchange_kernel,
        out_shape=jax.ShapeDtypeStruct(blocks.shape, blocks.dtype),
        in_specs=[whole],
        out_specs=whole,
        scratch_shapes=[
            pltpu.VMEM((chips - 1,) + blocks.shape[1:], blocks.dtype),
            pltpu.SemaphoreType.DMA((chips - 1,)),
            pltpu.SemaphoreType.DMA((chips - 1,)),
        ],
        compiler_params=pltpu.CompilerParams(collective_id=0, has_side_effects=True),
    )(blocks)


def _whole(shape):
    return pl.BlockSpec(shape, lambda i, *_: (0,) * len(shape))


def pack_document_runs(rows, starts, peer_count, capacity):
    out_shape = (peer_count, capacity) + rows.shape[1:]
    return pl.pallas_call(
        _pack_kernel,
        out_shape=jax.ShapeDtypeStruct(out_shape, rows.dtype),
        grid_spec=pltpu.PrefetchScalarGridSpec(
            num_scalar_prefetch=1,
            grid=(1,),
            in_specs=[_whole(rows.shape)],
            out_specs=_whole(out_shape),
        ),
    )(starts, rows)


def _unpack_kernel(index_ref, flat_ref, out_ref):
    def move_row(p, carry):
        out_ref[p] = flat_ref[index_ref[p]]
        return carry

    lax.fori_loop(0, out_ref.shape[0], move_row, 0, unroll=8)


def unpack_runs(flat_rows, index, row_count):
    out_shape = (row_count,) + flat_rows.shape[1:]
    return pl.pallas_call(
        _unpack_kernel,
        out_shape=jax.ShapeDtypeStruct(out_shape, flat_rows.dtype),
        grid_spec=pltpu.PrefetchScalarGridSpec(
            num_scalar_prefetch=1,
            grid=(1,),
            in_specs=[_whole(flat_rows.shape)],
            out_specs=_whole(out_shape),
        ),
    )(index, flat_rows)


def select_rows(rows, index):
    picks = (index[:, None] == jnp.arange(rows.shape[0], dtype=index.dtype)[None, :])
    return jnp.dot(
        picks.astype(rows.dtype), rows, preferred_element_type=jnp.float32
    ).astype(rows.dtype)


CTX = ("cx", "cc")


def on_device(
    input_entries, segment_entry_counts, segment_destination_part, norm_gain, kv_weight, kv_bias
):
    chips = lax.axis_size("cx")
    cores = lax.axis_size("cc")
    peer_count = chips * cores
    core = lax.axis_index("cc")
    myself = lax.axis_index("cx") * cores + core
    row_count = input_entries.shape[1]
    width = kv_weight.shape[0]
    heads_per_core = KVH // cores
    here = lax.axis_index("cx")

    block, kind, lane = jnp.unravel_index(
        jnp.arange(heads_per_core * 2 * HD, dtype=jnp.int32), (heads_per_core, 2, HD)
    )
    head = ((here + block) % heads_per_core) * cores + core
    columns = kind * KVH * HD + head * HD + lane
    picks = jnp.arange(kv_weight.shape[1], dtype=jnp.int32)[:, None] == columns[None, :]
    local_weight = jnp.dot(
        kv_weight, picks.astype(kv_weight.dtype), preferred_element_type=jnp.float32
    ).astype(kv_weight.dtype)
    local_bias = jnp.take(kv_bias, columns, mode="clip")
    local_weight, input_entries = lax.optimization_barrier((local_weight, input_entries))
    local_weight = with_layout_constraint(local_weight, Layout(major_to_minor=(0, 1)))
    gathered_weight = lax.all_gather(local_weight, "dp", axis=0, tiled=True)
    gathered_weight = with_layout_constraint(gathered_weight, Layout(major_to_minor=(0, 1)))

    counts, anchors, offsets, run_ends = plan_tables(
        segment_entry_counts[0], segment_destination_part[0], peer_count
    )
    positions = jnp.arange(row_count, dtype=jnp.int32)
    capacity = 2 * row_count // peer_count
    starts = window_starts(anchors, row_count, capacity)
    rows = input_entries[0]
    outgoing = select_rows(rows, (starts[myself][:, None] + jnp.arange(capacity)).reshape(-1))
    arriving_rows = lax.all_to_all(
        outgoing.reshape(peer_count, capacity, -1), CTX, split_axis=0, concat_axis=0, tiled=True
    )
    source, within, anchor = source_of(
        positions, run_ends[:, myself], offsets[:, myself], anchors[:, myself], peer_count
    )
    shift = anchor - jnp.take(starts[:, myself], source, mode="clip")
    index = source * capacity + shift + within
    local_bias, index = lax.optimization_barrier((local_bias, index))
    moved_rows = select_rows(arriving_rows.reshape(peer_count * capacity, -1), index)
    normed = rms_normed(moved_rows, norm_gain)
    sibling_rows = lax.ppermute(normed, "cc", perm=[(0, 1), (1, 0)])

    def project(rows):
        products = jnp.dot(rows, gathered_weight, preferred_element_type=jnp.float32)
        products = (products + local_bias[None, :]).astype(jnp.bfloat16)
        return jnp.swapaxes(products.reshape(row_count, heads_per_core, 2 * HD), 0, 1)

    own = project(normed)
    other = project(sibling_rows)
    first = jnp.where(core == 0, own, other)
    second = jnp.where(core == 0, other, own)
    mapped = jnp.concatenate([first, second], axis=1)
    by_heads = exchange_blocks(mapped).reshape(1, chips * cores * row_count, 2, 1, HD)
    return (moved_rows[None], by_heads)


def solution(mesh):
    dp_size, ctx_size = mesh.devices.shape
    cores = 2
    devices = np.asarray(mesh.devices).reshape(dp_size, ctx_size // cores, cores)
    split_mesh = Mesh(devices, ("dp", "cx", "cc"))
    in_specs = (
        P("dp", CTX, None),
        P("dp", None, None),
        P("dp", None, None),
        P(),
        P("dp", None),
        P(),
    )
    out_specs = (P("dp", CTX, None), P("dp", None, None, CTX, None))
    return jax.shard_map(
        on_device, mesh=split_mesh, in_specs=in_specs, out_specs=out_specs, check_vma=False
    )
```

```python
import jax
import jax.numpy as jnp
import numpy as np
from jax import lax
from jax.experimental import pallas as pl
from jax.experimental.pallas import tpu as pltpu
from jax.experimental.layout import Layout, with_layout_constraint
from jax.sharding import Mesh, PartitionSpec as P

KVH = 8
HD = 128


def plan_tables(lengths, targets, peer_count):
    labels = jnp.arange(peer_count, dtype=jnp.int32)
    starts = jnp.cumsum(lengths, axis=1) - lengths
    matches = (targets[:, :, None] == labels[None, None, :]).astype(jnp.int32)
    counts = jnp.sum(lengths[:, :, None] * matches, axis=1)
    anchors = jnp.sum(starts[:, :, None] * matches, axis=1)
    run_ends = jnp.cumsum(counts, axis=0)
    offsets = run_ends - counts
    return (counts, anchors, offsets, run_ends)


def source_of(positions, ends_column, offsets_column, anchors_column, peer_count):
    labels = jnp.arange(peer_count, dtype=jnp.int32)
    source = jnp.sum((ends_column[None, :] <= positions[:, None]).astype(jnp.int32), axis=1)
    chosen = (source[:, None] == labels[None, :]).astype(jnp.int32)
    within = positions - jnp.sum(chosen * offsets_column[None, :], axis=1)
    anchor = jnp.sum(chosen * anchors_column[None, :], axis=1)
    return (source, within, anchor)


def rms_normed(rows, norm_gain):
    as_float = rows.astype(jnp.float32)
    inverse_rms = lax.rsqrt(jnp.mean(as_float * as_float, axis=-1, keepdims=True) + 1e-06)
    return (as_float * inverse_rms * norm_gain[None, :]).astype(jnp.bfloat16)


def window_starts(anchors, row_count, capacity):
    return jnp.minimum(anchors, row_count - capacity)


def _pack_kernel(starts_ref, rows_ref, out_ref):
    peer_count, capacity = out_ref.shape[0], out_ref.shape[1]
    for k in range(peer_count):
        out_ref[k] = rows_ref[pl.ds(starts_ref[k], capacity)]


def _whole(shape):
    return pl.BlockSpec(shape, lambda i, *_: (0,) * len(shape))


def pack_document_runs(rows, starts, peer_count, capacity):
    out_shape = (peer_count, capacity) + rows.shape[1:]
    return pl.pallas_call(
        _pack_kernel,
        out_shape=jax.ShapeDtypeStruct(out_shape, rows.dtype),
        grid_spec=pltpu.PrefetchScalarGridSpec(
            num_scalar_prefetch=1,
            grid=(1,),
            in_specs=[_whole(rows.shape)],
            out_specs=_whole(out_shape),
        ),
    )(starts, rows)


def _unpack_kernel(index_ref, flat_ref, out_ref):
    def move_row(p, carry):
        out_ref[p] = flat_ref[index_ref[p]]
        return carry

    lax.fori_loop(0, out_ref.shape[0], move_row, 0, unroll=8)


def unpack_runs(flat_rows, index, row_count):
    out_shape = (row_count,) + flat_rows.shape[1:]
    return pl.pallas_call(
        _unpack_kernel,
        out_shape=jax.ShapeDtypeStruct(out_shape, flat_rows.dtype),
        grid_spec=pltpu.PrefetchScalarGridSpec(
            num_scalar_prefetch=1,
            grid=(1,),
            in_specs=[_whole(flat_rows.shape)],
            out_specs=_whole(out_shape),
        ),
    )(index, flat_rows)


def select_rows(rows, index):
    picks = (index[:, None] == jnp.arange(rows.shape[0], dtype=index.dtype)[None, :])
    return jnp.dot(
        picks.astype(rows.dtype), rows, preferred_element_type=jnp.float32
    ).astype(rows.dtype)


CTX = ("cx", "cc")


def on_device(
    input_entries, segment_entry_counts, segment_destination_part, norm_gain, kv_weight, kv_bias
):
    chips = lax.axis_size("cx")
    cores = lax.axis_size("cc")
    peer_count = chips * cores
    core = lax.axis_index("cc")
    myself = lax.axis_index("cx") * cores + core
    row_count = input_entries.shape[1]
    width = kv_weight.shape[0]
    heads_per_core = KVH // cores
    here = lax.axis_index("cx")

    block, kind, lane = jnp.unravel_index(
        jnp.arange(heads_per_core * 2 * HD, dtype=jnp.int32), (heads_per_core, 2, HD)
    )
    head = ((here + block) % heads_per_core) * cores + core
    columns = kind * KVH * HD + head * HD + lane
    picks = jnp.arange(kv_weight.shape[1], dtype=jnp.int32)[:, None] == columns[None, :]
    local_weight = jnp.dot(
        kv_weight, picks.astype(kv_weight.dtype), preferred_element_type=jnp.float32
    ).astype(kv_weight.dtype)
    local_bias = jnp.take(kv_bias, columns, mode="clip")
    local_weight, input_entries = lax.optimization_barrier((local_weight, input_entries))
    local_weight = with_layout_constraint(local_weight, Layout(major_to_minor=(0, 1)))
    gathered_weight = lax.all_gather(local_weight, "dp", axis=0, tiled=True)
    gathered_weight = with_layout_constraint(gathered_weight, Layout(major_to_minor=(0, 1)))

    counts, anchors, offsets, run_ends = plan_tables(
        segment_entry_counts[0], segment_destination_part[0], peer_count
    )
    positions = jnp.arange(row_count, dtype=jnp.int32)
    capacity = 2 * row_count // peer_count
    starts = window_starts(anchors, row_count, capacity)
    rows = input_entries[0]
    outgoing = select_rows(rows, (starts[myself][:, None] + jnp.arange(capacity)).reshape(-1))
    arriving_rows = lax.all_to_all(
        outgoing.reshape(peer_count, capacity, -1), CTX, split_axis=0, concat_axis=0, tiled=True
    )
    source, within, anchor = source_of(
        positions, run_ends[:, myself], offsets[:, myself], anchors[:, myself], peer_count
    )
    shift = anchor - jnp.take(starts[:, myself], source, mode="clip")
    index = source * capacity + shift + within
    local_bias, index = lax.optimization_barrier((local_bias, index))
    moved_rows = select_rows(arriving_rows.reshape(peer_count * capacity, -1), index)
    normed = rms_normed(moved_rows, norm_gain)
    sibling_rows = lax.ppermute(normed, "cc", perm=[(0, 1), (1, 0)])

    def project(rows):
        products = jnp.dot(rows, gathered_weight, preferred_element_type=jnp.float32)
        products = (products + local_bias[None, :]).astype(jnp.bfloat16)
        return jnp.swapaxes(products.reshape(row_count, heads_per_core, 2 * HD), 0, 1)

    by_heads = jnp.zeros((chips, cores, row_count, 2 * HD), kv_weight.dtype)

    def send_half(blocks, half, by_heads):
        by_heads = lax.dynamic_update_slice(by_heads, blocks[0][None, None], (here, half, 0, 0))
        for step in range(1, chips):
            arrived = lax.ppermute(
                blocks[step], "cx", perm=[(i, (i + step) % chips) for i in range(chips)]
            )
            source = (here + chips - step) % chips
            by_heads = lax.dynamic_update_slice(by_heads, arrived[None, None], (source, half, 0, 0))
        return by_heads

    own_blocks = project(normed)
    own_blocks, sibling_rows = lax.optimization_barrier((own_blocks, sibling_rows))
    by_heads = send_half(own_blocks, core, by_heads)
    by_heads = send_half(project(sibling_rows), 1 - core, by_heads)
    by_heads = by_heads.reshape(1, chips * cores * row_count, 2, 1, HD)
    return (moved_rows[None], by_heads)


def solution(mesh):
    dp_size, ctx_size = mesh.devices.shape
    cores = 2
    devices = np.asarray(mesh.devices).reshape(dp_size, ctx_size // cores, cores)
    split_mesh = Mesh(devices, ("dp", "cx", "cc"))
    in_specs = (
        P("dp", CTX, None),
        P("dp", None, None),
        P("dp", None, None),
        P(),
        P("dp", None),
        P(),
    )
    out_specs = (P("dp", CTX, None), P("dp", None, None, CTX, None))
    return jax.shard_map(
        on_device, mesh=split_mesh, in_specs=in_specs, out_specs=out_specs, check_vma=False
    )
```

```python
import jax
import jax.numpy as jnp
import numpy as np
from jax import lax
from jax.experimental import pallas as pl
from jax.experimental.pallas import tpu as pltpu
from jax.experimental.layout import Layout, with_layout_constraint
from jax.sharding import Mesh, PartitionSpec as P

KVH = 8
HD = 128


def plan_tables(lengths, targets, peer_count):
    labels = jnp.arange(peer_count, dtype=jnp.int32)
    starts = jnp.cumsum(lengths, axis=1) - lengths
    matches = (targets[:, :, None] == labels[None, None, :]).astype(jnp.int32)
    counts = jnp.sum(lengths[:, :, None] * matches, axis=1)
    anchors = jnp.sum(starts[:, :, None] * matches, axis=1)
    run_ends = jnp.cumsum(counts, axis=0)
    offsets = run_ends - counts
    return (counts, anchors, offsets, run_ends)


def source_of(positions, ends_column, offsets_column, anchors_column, peer_count):
    labels = jnp.arange(peer_count, dtype=jnp.int32)
    source = jnp.sum((ends_column[None, :] <= positions[:, None]).astype(jnp.int32), axis=1)
    chosen = (source[:, None] == labels[None, :]).astype(jnp.int32)
    within = positions - jnp.sum(chosen * offsets_column[None, :], axis=1)
    anchor = jnp.sum(chosen * anchors_column[None, :], axis=1)
    return (source, within, anchor)


def rms_normed(rows, norm_gain):
    as_float = rows.astype(jnp.float32)
    inverse_rms = lax.rsqrt(jnp.mean(as_float * as_float, axis=-1, keepdims=True) + 1e-06)
    return (as_float * inverse_rms * norm_gain[None, :]).astype(jnp.bfloat16)


def window_starts(anchors, row_count, capacity):
    return jnp.minimum(anchors, row_count - capacity)


def _pack_kernel(starts_ref, rows_ref, out_ref):
    peer_count, capacity = out_ref.shape[0], out_ref.shape[1]
    for k in range(peer_count):
        out_ref[k] = rows_ref[pl.ds(starts_ref[k], capacity)]


def _whole(shape):
    return pl.BlockSpec(shape, lambda i, *_: (0,) * len(shape))


def pack_document_runs(rows, starts, peer_count, capacity):
    out_shape = (peer_count, capacity) + rows.shape[1:]
    return pl.pallas_call(
        _pack_kernel,
        out_shape=jax.ShapeDtypeStruct(out_shape, rows.dtype),
        grid_spec=pltpu.PrefetchScalarGridSpec(
            num_scalar_prefetch=1,
            grid=(1,),
            in_specs=[_whole(rows.shape)],
            out_specs=_whole(out_shape),
        ),
    )(starts, rows)


def _unpack_kernel(index_ref, flat_ref, out_ref):
    def move_row(p, carry):
        out_ref[p] = flat_ref[index_ref[p]]
        return carry

    lax.fori_loop(0, out_ref.shape[0], move_row, 0, unroll=8)


def unpack_runs(flat_rows, index, row_count):
    out_shape = (row_count,) + flat_rows.shape[1:]
    return pl.pallas_call(
        _unpack_kernel,
        out_shape=jax.ShapeDtypeStruct(out_shape, flat_rows.dtype),
        grid_spec=pltpu.PrefetchScalarGridSpec(
            num_scalar_prefetch=1,
            grid=(1,),
            in_specs=[_whole(flat_rows.shape)],
            out_specs=_whole(out_shape),
        ),
    )(index, flat_rows)


def select_rows(rows, index):
    picks = (index[:, None] == jnp.arange(rows.shape[0], dtype=index.dtype)[None, :])
    return jnp.dot(
        picks.astype(rows.dtype), rows, preferred_element_type=jnp.float32
    ).astype(rows.dtype)


CTX = ("cx", "cc")


def on_device(
    input_entries, segment_entry_counts, segment_destination_part, norm_gain, kv_weight, kv_bias
):
    chips = lax.axis_size("cx")
    cores = lax.axis_size("cc")
    peer_count = chips * cores
    core = lax.axis_index("cc")
    myself = lax.axis_index("cx") * cores + core
    row_count = input_entries.shape[1]
    width = kv_weight.shape[0]
    heads_per_core = KVH // cores
    here = lax.axis_index("cx")

    block, kind, lane = jnp.unravel_index(
        jnp.arange(heads_per_core * 2 * HD, dtype=jnp.int32), (heads_per_core, 2, HD)
    )
    head = ((here + block) % heads_per_core) * cores + core
    columns = kind * KVH * HD + head * HD + lane
    picks = jnp.arange(kv_weight.shape[1], dtype=jnp.int32)[:, None] == columns[None, :]
    local_weight = jnp.dot(
        kv_weight, picks.astype(kv_weight.dtype), preferred_element_type=jnp.float32
    ).astype(kv_weight.dtype)
    local_bias = jnp.take(kv_bias, columns, mode="clip")
    local_weight, input_entries = lax.optimization_barrier((local_weight, input_entries))
    local_weight = with_layout_constraint(local_weight, Layout(major_to_minor=(0, 1)))
    gathered_weight = lax.all_gather(local_weight, "dp", axis=0, tiled=True)
    gathered_weight = with_layout_constraint(gathered_weight, Layout(major_to_minor=(0, 1)))

    counts, anchors, offsets, run_ends = plan_tables(
        segment_entry_counts[0], segment_destination_part[0], peer_count
    )
    positions = jnp.arange(row_count, dtype=jnp.int32)
    capacity = 2 * row_count // peer_count
    starts = window_starts(anchors, row_count, capacity)
    rows = input_entries[0]
    outgoing = select_rows(rows, (starts[myself][:, None] + jnp.arange(capacity)).reshape(-1))
    arriving_rows = lax.all_to_all(
        outgoing.reshape(peer_count, capacity, -1), CTX, split_axis=0, concat_axis=0, tiled=True
    )
    source, within, anchor = source_of(
        positions, run_ends[:, myself], offsets[:, myself], anchors[:, myself], peer_count
    )
    shift = anchor - jnp.take(starts[:, myself], source, mode="clip")
    index = source * capacity + shift + within
    local_bias, index = lax.optimization_barrier((local_bias, index))
    moved_rows = select_rows(arriving_rows.reshape(peer_count * capacity, -1), index)
    as_float = moved_rows.astype(jnp.float32)
    inverse_rms = lax.rsqrt(jnp.mean(as_float * as_float, axis=-1, keepdims=True) + 1e-06)
    gathered_weight, inverse_rms = lax.optimization_barrier((gathered_weight, inverse_rms))
    normed = (as_float * inverse_rms * norm_gain[None, :]).astype(jnp.bfloat16)
    sibling_rows = lax.ppermute(normed, "cc", perm=[(0, 1), (1, 0)])

    def project(rows):
        products = jnp.dot(rows, gathered_weight, preferred_element_type=jnp.float32)
        products = (products + local_bias[None, :]).astype(jnp.bfloat16)
        return jnp.swapaxes(products.reshape(row_count, heads_per_core, 2 * HD), 0, 1)

    by_heads = jnp.zeros((chips, cores, row_count, 2 * HD), kv_weight.dtype)

    def send_half(blocks, half, by_heads):
        by_heads = lax.dynamic_update_slice(by_heads, blocks[0][None, None], (here, half, 0, 0))
        for step in range(1, chips):
            arrived = lax.ppermute(
                blocks[step], "cx", perm=[(i, (i + step) % chips) for i in range(chips)]
            )
            source = (here + chips - step) % chips
            by_heads = lax.dynamic_update_slice(by_heads, arrived[None, None], (source, half, 0, 0))
        return by_heads

    own_blocks = project(normed)
    own_blocks, sibling_rows = lax.optimization_barrier((own_blocks, sibling_rows))
    by_heads = send_half(own_blocks, core, by_heads)
    by_heads = send_half(project(sibling_rows), 1 - core, by_heads)
    by_heads = by_heads.reshape(1, chips * cores * row_count, 2, 1, HD)
    return (moved_rows[None], by_heads)


def solution(mesh):
    dp_size, ctx_size = mesh.devices.shape
    cores = 2
    devices = np.asarray(mesh.devices).reshape(dp_size, ctx_size // cores, cores)
    split_mesh = Mesh(devices, ("dp", "cx", "cc"))
    in_specs = (
        P("dp", CTX, None),
        P("dp", None, None),
        P("dp", None, None),
        P(),
        P("dp", None),
        P(),
    )
    out_specs = (P("dp", CTX, None), P("dp", None, None, CTX, None))
    return jax.shard_map(
        on_device, mesh=split_mesh, in_specs=in_specs, out_specs=out_specs, check_vma=False
    )
```

```python
import jax
import jax.numpy as jnp
import numpy as np
from jax import lax
from jax.experimental import pallas as pl
from jax.experimental.pallas import tpu as pltpu
from jax.experimental.layout import Layout, with_layout_constraint
from jax.sharding import Mesh, PartitionSpec as P

KVH = 8
HD = 128


def plan_tables(lengths, targets, peer_count):
    labels = jnp.arange(peer_count, dtype=jnp.int32)
    starts = jnp.cumsum(lengths, axis=1) - lengths
    matches = (targets[:, :, None] == labels[None, None, :]).astype(jnp.int32)
    counts = jnp.sum(lengths[:, :, None] * matches, axis=1)
    anchors = jnp.sum(starts[:, :, None] * matches, axis=1)
    run_ends = jnp.cumsum(counts, axis=0)
    offsets = run_ends - counts
    return (counts, anchors, offsets, run_ends)


def source_of(positions, ends_column, offsets_column, anchors_column, peer_count):
    labels = jnp.arange(peer_count, dtype=jnp.int32)
    source = jnp.sum((ends_column[None, :] <= positions[:, None]).astype(jnp.int32), axis=1)
    chosen = (source[:, None] == labels[None, :]).astype(jnp.int32)
    within = positions - jnp.sum(chosen * offsets_column[None, :], axis=1)
    anchor = jnp.sum(chosen * anchors_column[None, :], axis=1)
    return (source, within, anchor)


def rms_normed(rows, norm_gain):
    as_float = rows.astype(jnp.float32)
    inverse_rms = lax.rsqrt(jnp.mean(as_float * as_float, axis=-1, keepdims=True) + 1e-06)
    return (as_float * inverse_rms * norm_gain[None, :]).astype(jnp.bfloat16)


def window_starts(anchors, row_count, capacity):
    return jnp.minimum(anchors, row_count - capacity)


def _pack_kernel(starts_ref, rows_ref, out_ref):
    peer_count, capacity = out_ref.shape[0], out_ref.shape[1]
    for k in range(peer_count):
        out_ref[k] = rows_ref[pl.ds(starts_ref[k], capacity)]


def _whole(shape):
    return pl.BlockSpec(shape, lambda i, *_: (0,) * len(shape))


def pack_document_runs(rows, starts, peer_count, capacity):
    out_shape = (peer_count, capacity) + rows.shape[1:]
    return pl.pallas_call(
        _pack_kernel,
        out_shape=jax.ShapeDtypeStruct(out_shape, rows.dtype),
        grid_spec=pltpu.PrefetchScalarGridSpec(
            num_scalar_prefetch=1,
            grid=(1,),
            in_specs=[_whole(rows.shape)],
            out_specs=_whole(out_shape),
        ),
    )(starts, rows)


def _unpack_kernel(index_ref, flat_ref, out_ref):
    def move_row(p, carry):
        out_ref[p] = flat_ref[index_ref[p]]
        return carry

    lax.fori_loop(0, out_ref.shape[0], move_row, 0, unroll=8)


def unpack_runs(flat_rows, index, row_count):
    out_shape = (row_count,) + flat_rows.shape[1:]
    return pl.pallas_call(
        _unpack_kernel,
        out_shape=jax.ShapeDtypeStruct(out_shape, flat_rows.dtype),
        grid_spec=pltpu.PrefetchScalarGridSpec(
            num_scalar_prefetch=1,
            grid=(1,),
            in_specs=[_whole(flat_rows.shape)],
            out_specs=_whole(out_shape),
        ),
    )(index, flat_rows)


def select_rows(rows, index):
    picks = (index[:, None] == jnp.arange(rows.shape[0], dtype=index.dtype)[None, :])
    return jnp.dot(
        picks.astype(rows.dtype), rows, preferred_element_type=jnp.float32
    ).astype(rows.dtype)


CTX = ("cx", "cc")


def on_device(
    input_entries, segment_entry_counts, segment_destination_part, norm_gain, kv_weight, kv_bias
):
    chips = lax.axis_size("cx")
    cores = lax.axis_size("cc")
    peer_count = chips * cores
    core = lax.axis_index("cc")
    myself = lax.axis_index("cx") * cores + core
    row_count = input_entries.shape[1]
    width = kv_weight.shape[0]
    heads_per_core = KVH // cores
    here = lax.axis_index("cx")

    block, kind, lane = jnp.unravel_index(
        jnp.arange(heads_per_core * 2 * HD, dtype=jnp.int32), (heads_per_core, 2, HD)
    )
    head = ((here + block) % heads_per_core) * cores + core
    columns = kind * KVH * HD + head * HD + lane
    picks = jnp.arange(kv_weight.shape[1], dtype=jnp.int32)[:, None] == columns[None, :]
    local_weight = jnp.dot(
        kv_weight, picks.astype(kv_weight.dtype), preferred_element_type=jnp.float32
    ).astype(kv_weight.dtype)
    local_bias = jnp.take(kv_bias, columns, mode="clip")
    local_weight, input_entries = lax.optimization_barrier((local_weight, input_entries))
    local_weight = with_layout_constraint(local_weight, Layout(major_to_minor=(0, 1)))
    gathered_weight = lax.all_gather(local_weight, "dp", axis=0, tiled=True)
    gathered_weight = with_layout_constraint(gathered_weight, Layout(major_to_minor=(0, 1)))

    counts, anchors, offsets, run_ends = plan_tables(
        segment_entry_counts[0], segment_destination_part[0], peer_count
    )
    positions = jnp.arange(row_count, dtype=jnp.int32)
    capacity = 2 * row_count // peer_count
    starts = window_starts(anchors, row_count, capacity)
    rows = input_entries[0]
    my_starts = starts[myself]
    outgoing = jnp.concatenate(
        [lax.dynamic_slice_in_dim(rows, my_starts[k], capacity, axis=0) for k in range(peer_count)],
        axis=0,
    )
    arriving_rows = lax.all_to_all(
        outgoing.reshape(peer_count, capacity, -1), CTX, split_axis=0, concat_axis=0, tiled=True
    )
    source, within, anchor = source_of(
        positions, run_ends[:, myself], offsets[:, myself], anchors[:, myself], peer_count
    )
    shift = anchor - jnp.take(starts[:, myself], source, mode="clip")
    index = source * capacity + shift + within
    local_bias, index = lax.optimization_barrier((local_bias, index))
    moved_rows = select_rows(arriving_rows.reshape(peer_count * capacity, -1), index)
    normed = rms_normed(moved_rows, norm_gain)
    sibling_rows = lax.ppermute(normed, "cc", perm=[(0, 1), (1, 0)])

    def project(rows):
        products = jnp.dot(rows, gathered_weight, preferred_element_type=jnp.float32)
        products = (products + local_bias[None, :]).astype(jnp.bfloat16)
        return jnp.swapaxes(products.reshape(row_count, heads_per_core, 2 * HD), 0, 1)

    by_heads = jnp.zeros((chips, cores, row_count, 2 * HD), kv_weight.dtype)

    def send_half(blocks, half, by_heads):
        by_heads = lax.dynamic_update_slice(by_heads, blocks[0][None, None], (here, half, 0, 0))
        for step in range(1, chips):
            arrived = lax.ppermute(
                blocks[step], "cx", perm=[(i, (i + step) % chips) for i in range(chips)]
            )
            source = (here + chips - step) % chips
            by_heads = lax.dynamic_update_slice(by_heads, arrived[None, None], (source, half, 0, 0))
        return by_heads

    own_blocks = project(normed)
    own_blocks, sibling_rows = lax.optimization_barrier((own_blocks, sibling_rows))
    by_heads = send_half(own_blocks, core, by_heads)
    by_heads = send_half(project(sibling_rows), 1 - core, by_heads)
    by_heads = by_heads.reshape(1, chips * cores * row_count, 2, 1, HD)
    return (moved_rows[None], by_heads)


def solution(mesh):
    dp_size, ctx_size = mesh.devices.shape
    cores = 2
    devices = np.asarray(mesh.devices).reshape(dp_size, ctx_size // cores, cores)
    split_mesh = Mesh(devices, ("dp", "cx", "cc"))
    in_specs = (
        P("dp", CTX, None),
        P("dp", None, None),
        P("dp", None, None),
        P(),
        P("dp", None),
        P(),
    )
    out_specs = (P("dp", CTX, None), P("dp", None, None, CTX, None))
    return jax.shard_map(
        on_device, mesh=split_mesh, in_specs=in_specs, out_specs=out_specs, check_vma=False
    )
```

```python
import jax
import jax.numpy as jnp
import numpy as np
from jax import lax
from jax.experimental import pallas as pl
from jax.experimental.pallas import tpu as pltpu
from jax.experimental.layout import Layout, with_layout_constraint
from jax.sharding import Mesh, PartitionSpec as P

KVH = 8
HD = 128


def plan_tables(lengths, targets, peer_count):
    labels = jnp.arange(peer_count, dtype=jnp.int32)
    starts = jnp.cumsum(lengths, axis=1) - lengths
    matches = (targets[:, :, None] == labels[None, None, :]).astype(jnp.int32)
    counts = jnp.sum(lengths[:, :, None] * matches, axis=1)
    anchors = jnp.sum(starts[:, :, None] * matches, axis=1)
    run_ends = jnp.cumsum(counts, axis=0)
    offsets = run_ends - counts
    return (counts, anchors, offsets, run_ends)


def source_of(positions, ends_column, offsets_column, anchors_column, peer_count):
    labels = jnp.arange(peer_count, dtype=jnp.int32)
    source = jnp.sum((ends_column[None, :] <= positions[:, None]).astype(jnp.int32), axis=1)
    chosen = (source[:, None] == labels[None, :]).astype(jnp.int32)
    within = positions - jnp.sum(chosen * offsets_column[None, :], axis=1)
    anchor = jnp.sum(chosen * anchors_column[None, :], axis=1)
    return (source, within, anchor)


def rms_normed(rows, norm_gain):
    as_float = rows.astype(jnp.float32)
    inverse_rms = lax.rsqrt(jnp.mean(as_float * as_float, axis=-1, keepdims=True) + 1e-06)
    return (as_float * inverse_rms * norm_gain[None, :]).astype(jnp.bfloat16)


def window_starts(anchors, row_count, capacity):
    return jnp.minimum(anchors, row_count - capacity)


def _pack_kernel(starts_ref, rows_ref, out_ref):
    peer_count, capacity = out_ref.shape[0], out_ref.shape[1]
    for k in range(peer_count):
        out_ref[k] = rows_ref[pl.ds(starts_ref[k], capacity)]


def _whole(shape):
    return pl.BlockSpec(shape, lambda i, *_: (0,) * len(shape))


def pack_document_runs(rows, starts, peer_count, capacity):
    out_shape = (peer_count, capacity) + rows.shape[1:]
    return pl.pallas_call(
        _pack_kernel,
        out_shape=jax.ShapeDtypeStruct(out_shape, rows.dtype),
        grid_spec=pltpu.PrefetchScalarGridSpec(
            num_scalar_prefetch=1,
            grid=(1,),
            in_specs=[_whole(rows.shape)],
            out_specs=_whole(out_shape),
        ),
    )(starts, rows)


def _unpack_kernel(index_ref, flat_ref, out_ref):
    def move_row(p, carry):
        out_ref[p] = flat_ref[index_ref[p]]
        return carry

    lax.fori_loop(0, out_ref.shape[0], move_row, 0, unroll=8)


def unpack_runs(flat_rows, index, row_count):
    out_shape = (row_count,) + flat_rows.shape[1:]
    return pl.pallas_call(
        _unpack_kernel,
        out_shape=jax.ShapeDtypeStruct(out_shape, flat_rows.dtype),
        grid_spec=pltpu.PrefetchScalarGridSpec(
            num_scalar_prefetch=1,
            grid=(1,),
            in_specs=[_whole(flat_rows.shape)],
            out_specs=_whole(out_shape),
        ),
    )(index, flat_rows)


def select_rows(rows, index):
    picks = (index[:, None] == jnp.arange(rows.shape[0], dtype=index.dtype)[None, :])
    return jnp.dot(
        picks.astype(rows.dtype), rows, preferred_element_type=jnp.float32
    ).astype(rows.dtype)


CTX = ("cx", "cc")


def on_device(
    input_entries, segment_entry_counts, segment_destination_part, norm_gain, kv_weight, kv_bias
):
    chips = lax.axis_size("cx")
    cores = lax.axis_size("cc")
    peer_count = chips * cores
    core = lax.axis_index("cc")
    myself = lax.axis_index("cx") * cores + core
    row_count = input_entries.shape[1]
    width = kv_weight.shape[0]
    heads_per_core = KVH // cores
    here = lax.axis_index("cx")

    block, kind, lane = jnp.unravel_index(
        jnp.arange(heads_per_core * 2 * HD, dtype=jnp.int32), (heads_per_core, 2, HD)
    )
    head = ((here + block) % heads_per_core) * cores + core
    columns = kind * KVH * HD + head * HD + lane
    picks = jnp.arange(kv_weight.shape[1], dtype=jnp.int32)[:, None] == columns[None, :]
    local_weight = jnp.dot(
        kv_weight, picks.astype(kv_weight.dtype), preferred_element_type=jnp.float32
    ).astype(kv_weight.dtype)
    local_bias = jnp.take(kv_bias, columns, mode="clip")
    local_weight, input_entries = lax.optimization_barrier((local_weight, input_entries))
    local_weight = with_layout_constraint(local_weight, Layout(major_to_minor=(0, 1)))
    gathered_weight = lax.all_gather(local_weight, "dp", axis=0, tiled=True)
    gathered_weight = with_layout_constraint(gathered_weight, Layout(major_to_minor=(0, 1)))

    counts, anchors, offsets, run_ends = plan_tables(
        segment_entry_counts[0], segment_destination_part[0], peer_count
    )
    positions = jnp.arange(row_count, dtype=jnp.int32)
    capacity = 2 * row_count // peer_count
    starts = window_starts(anchors, row_count, capacity)
    rows = input_entries[0]
    outgoing = select_rows(rows, (starts[myself][:, None] + jnp.arange(capacity)).reshape(-1))
    arriving_rows = lax.all_to_all(
        outgoing.reshape(peer_count, capacity, -1), CTX, split_axis=0, concat_axis=0, tiled=True
    )
    source, within, anchor = source_of(
        positions, run_ends[:, myself], offsets[:, myself], anchors[:, myself], peer_count
    )
    shift = anchor - jnp.take(starts[:, myself], source, mode="clip")
    index = source * capacity + shift + within
    local_bias, index = lax.optimization_barrier((local_bias, index))
    moved_rows = select_rows(arriving_rows.reshape(peer_count * capacity, -1), index)
    normed = rms_normed(moved_rows, norm_gain)
    sibling_rows = lax.ppermute(normed, "cc", perm=[(0, 1), (1, 0)])

    def project(rows):
        products = jnp.dot(rows, gathered_weight, preferred_element_type=jnp.float32)
        products = (products + local_bias[None, :]).astype(jnp.bfloat16)
        return jnp.swapaxes(products.reshape(row_count, heads_per_core, 2 * HD), 0, 1)

    by_heads = jnp.zeros((chips, cores, row_count, 2 * HD), kv_weight.dtype)

    def send_half(blocks, half, by_heads):
        by_heads = lax.dynamic_update_slice(by_heads, blocks[0][None, None], (here, half, 0, 0))
        for step in sorted(range(1, chips), key=lambda d: -min(d, chips - d)):
            arrived = lax.ppermute(
                blocks[step], "cx", perm=[(i, (i + step) % chips) for i in range(chips)]
            )
            source = (here + chips - step) % chips
            by_heads = lax.dynamic_update_slice(by_heads, arrived[None, None], (source, half, 0, 0))
        return by_heads

    own_blocks = project(normed)
    own_blocks, sibling_rows = lax.optimization_barrier((own_blocks, sibling_rows))
    by_heads = send_half(own_blocks, core, by_heads)
    by_heads = send_half(project(sibling_rows), 1 - core, by_heads)
    by_heads = by_heads.reshape(1, chips * cores * row_count, 2, 1, HD)
    return (moved_rows[None], by_heads)


def solution(mesh):
    dp_size, ctx_size = mesh.devices.shape
    cores = 2
    devices = np.asarray(mesh.devices).reshape(dp_size, ctx_size // cores, cores)
    split_mesh = Mesh(devices, ("dp", "cx", "cc"))
    in_specs = (
        P("dp", CTX, None),
        P("dp", None, None),
        P("dp", None, None),
        P(),
        P("dp", None),
        P(),
    )
    out_specs = (P("dp", CTX, None), P("dp", None, None, CTX, None))
    return jax.shard_map(
        on_device, mesh=split_mesh, in_specs=in_specs, out_specs=out_specs, check_vma=False
    )
```

```python
import jax
import jax.numpy as jnp
import numpy as np
from jax import lax
from jax.experimental import pallas as pl
from jax.experimental.pallas import tpu as pltpu
from jax.experimental.layout import Layout, with_layout_constraint
from jax.sharding import Mesh, PartitionSpec as P

KVH = 8
HD = 128


def plan_tables(lengths, targets, peer_count):
    labels = jnp.arange(peer_count, dtype=jnp.int32)
    starts = jnp.cumsum(lengths, axis=1) - lengths
    matches = (targets[:, :, None] == labels[None, None, :]).astype(jnp.int32)
    counts = jnp.sum(lengths[:, :, None] * matches, axis=1)
    anchors = jnp.sum(starts[:, :, None] * matches, axis=1)
    run_ends = jnp.cumsum(counts, axis=0)
    offsets = run_ends - counts
    return (counts, anchors, offsets, run_ends)


def source_of(positions, ends_column, offsets_column, anchors_column, peer_count):
    labels = jnp.arange(peer_count, dtype=jnp.int32)
    source = jnp.sum((ends_column[None, :] <= positions[:, None]).astype(jnp.int32), axis=1)
    chosen = (source[:, None] == labels[None, :]).astype(jnp.int32)
    within = positions - jnp.sum(chosen * offsets_column[None, :], axis=1)
    anchor = jnp.sum(chosen * anchors_column[None, :], axis=1)
    return (source, within, anchor)


def rms_normed(rows, norm_gain):
    as_float = rows.astype(jnp.float32)
    inverse_rms = lax.rsqrt(jnp.mean(as_float * as_float, axis=-1, keepdims=True) + 1e-06)
    return (as_float * inverse_rms * norm_gain[None, :]).astype(jnp.bfloat16)


def window_starts(anchors, row_count, capacity):
    return jnp.minimum(anchors, row_count - capacity)


def _pack_kernel(starts_ref, rows_ref, out_ref):
    peer_count, capacity = out_ref.shape[0], out_ref.shape[1]
    for k in range(peer_count):
        out_ref[k] = rows_ref[pl.ds(starts_ref[k], capacity)]


def _whole(shape):
    return pl.BlockSpec(shape, lambda i, *_: (0,) * len(shape))


def pack_document_runs(rows, starts, peer_count, capacity):
    out_shape = (peer_count, capacity) + rows.shape[1:]
    return pl.pallas_call(
        _pack_kernel,
        out_shape=jax.ShapeDtypeStruct(out_shape, rows.dtype),
        grid_spec=pltpu.PrefetchScalarGridSpec(
            num_scalar_prefetch=1,
            grid=(1,),
            in_specs=[_whole(rows.shape)],
            out_specs=_whole(out_shape),
        ),
    )(starts, rows)


def _unpack_kernel(index_ref, flat_ref, out_ref):
    def move_row(p, carry):
        out_ref[p] = flat_ref[index_ref[p]]
        return carry

    lax.fori_loop(0, out_ref.shape[0], move_row, 0, unroll=8)


def unpack_runs(flat_rows, index, row_count):
    out_shape = (row_count,) + flat_rows.shape[1:]
    return pl.pallas_call(
        _unpack_kernel,
        out_shape=jax.ShapeDtypeStruct(out_shape, flat_rows.dtype),
        grid_spec=pltpu.PrefetchScalarGridSpec(
            num_scalar_prefetch=1,
            grid=(1,),
            in_specs=[_whole(flat_rows.shape)],
            out_specs=_whole(out_shape),
        ),
    )(index, flat_rows)


def select_rows(rows, index):
    picks = (index[:, None] == jnp.arange(rows.shape[0], dtype=index.dtype)[None, :])
    return jnp.dot(
        picks.astype(rows.dtype), rows, preferred_element_type=jnp.float32
    ).astype(rows.dtype)


CTX = ("cx", "cc")


def on_device(
    input_entries, segment_entry_counts, segment_destination_part, norm_gain, kv_weight, kv_bias
):
    chips = lax.axis_size("cx")
    cores = lax.axis_size("cc")
    peer_count = chips * cores
    core = lax.axis_index("cc")
    myself = lax.axis_index("cx") * cores + core
    row_count = input_entries.shape[1]
    width = kv_weight.shape[0]
    heads_per_core = KVH // cores
    here = lax.axis_index("cx")

    block, kind, lane = jnp.unravel_index(
        jnp.arange(heads_per_core * 2 * HD, dtype=jnp.int32), (heads_per_core, 2, HD)
    )
    head = ((here + block) % heads_per_core) * cores + core
    columns = kind * KVH * HD + head * HD + lane
    picks = jnp.arange(kv_weight.shape[1], dtype=jnp.int32)[:, None] == columns[None, :]
    local_weight = jnp.dot(
        kv_weight, picks.astype(kv_weight.dtype), preferred_element_type=jnp.float32
    ).astype(kv_weight.dtype)
    local_bias = jnp.take(kv_bias, columns, mode="clip")
    local_weight, input_entries = lax.optimization_barrier((local_weight, input_entries))
    local_weight = with_layout_constraint(local_weight, Layout(major_to_minor=(0, 1)))
    gathered_weight = lax.all_gather(local_weight, "dp", axis=0, tiled=True)
    gathered_weight = with_layout_constraint(gathered_weight, Layout(major_to_minor=(0, 1)))

    counts, anchors, offsets, run_ends = plan_tables(
        segment_entry_counts[0], segment_destination_part[0], peer_count
    )
    positions = jnp.arange(row_count, dtype=jnp.int32)
    capacity = 2 * row_count // peer_count
    starts = window_starts(anchors, row_count, capacity)
    rows = input_entries[0]
    outgoing = select_rows(rows, (starts[myself][:, None] + jnp.arange(capacity)).reshape(-1))
    arriving_rows = lax.all_to_all(
        outgoing.reshape(peer_count, capacity, -1), CTX, split_axis=0, concat_axis=0, tiled=True
    )
    source, within, anchor = source_of(
        positions, run_ends[:, myself], offsets[:, myself], anchors[:, myself], peer_count
    )
    shift = anchor - jnp.take(starts[:, myself], source, mode="clip")
    index = source * capacity + shift + within
    local_bias, index = lax.optimization_barrier((local_bias, index))
    moved_rows = select_rows(arriving_rows.reshape(peer_count * capacity, -1), index)
    normed = rms_normed(moved_rows, norm_gain)
    split = row_count // 2
    sibling_rows = jnp.concatenate(
        [lax.ppermute(normed[:split], "cc", perm=[(0, 1), (1, 0)]),
         lax.ppermute(normed[split:], "cc", perm=[(0, 1), (1, 0)])],
        axis=0,
    )

    def project(rows):
        products = jnp.dot(rows, gathered_weight, preferred_element_type=jnp.float32)
        products = (products + local_bias[None, :]).astype(jnp.bfloat16)
        return jnp.swapaxes(products.reshape(row_count, heads_per_core, 2 * HD), 0, 1)

    by_heads = jnp.zeros((chips, cores, row_count, 2 * HD), kv_weight.dtype)

    def send_half(blocks, half, by_heads):
        by_heads = lax.dynamic_update_slice(by_heads, blocks[0][None, None], (here, half, 0, 0))
        for step in sorted(range(1, chips), key=lambda d: -min(d, chips - d)):
            arrived = lax.ppermute(
                blocks[step], "cx", perm=[(i, (i + step) % chips) for i in range(chips)]
            )
            source = (here + chips - step) % chips
            by_heads = lax.dynamic_update_slice(by_heads, arrived[None, None], (source, half, 0, 0))
        return by_heads

    own_blocks = project(normed)
    own_blocks, sibling_rows = lax.optimization_barrier((own_blocks, sibling_rows))
    by_heads = send_half(own_blocks, core, by_heads)
    by_heads = send_half(project(sibling_rows), 1 - core, by_heads)
    by_heads = by_heads.reshape(1, chips * cores * row_count, 2, 1, HD)
    return (moved_rows[None], by_heads)


def solution(mesh):
    dp_size, ctx_size = mesh.devices.shape
    cores = 2
    devices = np.asarray(mesh.devices).reshape(dp_size, ctx_size // cores, cores)
    split_mesh = Mesh(devices, ("dp", "cx", "cc"))
    in_specs = (
        P("dp", CTX, None),
        P("dp", None, None),
        P("dp", None, None),
        P(),
        P("dp", None),
        P(),
    )
    out_specs = (P("dp", CTX, None), P("dp", None, None, CTX, None))
    return jax.shard_map(
        on_device, mesh=split_mesh, in_specs=in_specs, out_specs=out_specs, check_vma=False
    )
```
